256 devices in a mesh: sa: 4 (over y), row: 4 (over x), col: 16 (over z, core).
Axes of the slice: x: 4, y: 4, z: 8, core: 2. Of those that a mesh axis runs over, the one named last changes fastest.
Arguments:
- states: float32 [2560, 1024], P(None, 'sa')
- pool: float32 [32768, 1024], P(('row', 'col'), 'sa')
- pick: int32 [16384], P(('row', 'col')), may hold values from 0 to 32767, as said below
- tile_table: int32 [8256, 2], P(('row', 'col')), may hold values from 0 to 127, as said below
Outputs:
- normal_tiles: float32 [8256, 128, 128], P(('row', 'col'), 'sa')
The draws below stay inside these ranges and needn't reach their ends.
Inputs may be any that keep to these rules, and one draw needn't show every extreme that they name: pick[m] lies in pool rows 2 * 256 * (m // 256) to 2 * 256 * (m // 256 + 1) - 1, and the picks of one such group of 256 centres are distinct. `tile_table`: each row (i, j) has i <= j; every such pair of blocks appears in exactly one row; a row stored on the device at index r of row and c of col names one block whose centres lie on a device at row index r and another whose centres lie on a device at col index c.
All inputs are finite; a program needn't handle non-finite values.
Results may differ from the reference program's by a relative error of at most 0.00033.
Values may be sent and summed in bfloat16 or wider, within the bound.
A program may use at most 128 MiB of HBM per device.

```python
import math
import jax
import jax.numpy as jnp
import numpy as np
from jax import lax

F = 1024
M = 16384
MB = 128
SAMPLES = 2560
BLOCKS = 128
TILES = 8256
CENT_DEV = 256
POOL = 32768
N_COL = 16


def feature_scales(key):
    strong = max(F // 6, 1)
    strong_var = 0.95 * F / strong
    weak_var = 0.05 * F / (F - strong)
    ranks = jax.random.permutation(jax.random.fold_in(key, 16), F)
    chosen = jnp.where(ranks < strong, strong_var, weak_var)
    return jnp.sqrt(chosen.astype(jnp.float32))


def state_values(key, count, scales):
    magnitude_key, sign_key = jax.random.split(key)
    lower, upper = (0.7, 1.3)
    mean_square = (upper ** 3 - lower ** 3) / (3.0 * (upper - lower))
    magnitude = jax.random.uniform(magnitude_key, (count, F), jnp.float32, lower, upper) / math.sqrt(mean_square)
    signs = jnp.where(jax.random.bernoulli(sign_key, 0.5, (count, F)), 1.0, -1.0).astype(jnp.float32)
    return (magnitude * signs * scales[None, :]).astype(jnp.float32)


def draw_states(key, part):
    scales = feature_scales(key)
    return state_values(jax.random.fold_in(key, 11), SAMPLES, scales)


def draw_pool(key, part):
    scales = feature_scales(key)
    return state_values(jax.random.fold_in(key, 12), POOL, scales)


def group_pick(group_key):
    inner_key, order_key = jax.random.split(group_key)
    inner = jax.random.permutation(inner_key, 2 * CENT_DEV - 2)[:CENT_DEV - 2].astype(jnp.int32) + 1
    ends = jnp.array([0, 2 * CENT_DEV - 1], jnp.int32)
    return jax.random.permutation(order_key, jnp.concatenate([ends, inner]))


def draw_pick(key, part):
    owners = M // CENT_DEV
    owner_keys = jax.random.split(jax.random.fold_in(key, 13), owners)
    chosen = jax.vmap(group_pick)(owner_keys)
    offsets = jnp.arange(owners, dtype=jnp.int32)[:, None] * (2 * CENT_DEV)
    return (chosen.astype(jnp.int32) + offsets).reshape(M)


def draw_tile_table(key, part):
    upper_rows, upper_cols = np.triu_indices(BLOCKS)
    first = jnp.asarray(upper_rows, jnp.int32)
    second = jnp.asarray(upper_cols, jnp.int32)
    per_device = CENT_DEV // MB
    flips = jax.random.randint(jax.random.fold_in(key, 15), (BLOCKS, BLOCKS // 2), 0, 2, jnp.int32)
    flip = flips[first, second // 2]
    device_a = first // per_device
    device_b = second // per_device
    to_first = ((first + second) % 2 + flip) % 2 == 0
    cell_a = device_a // N_COL * N_COL + device_b % N_COL
    cell_b = device_b // N_COL * N_COL + device_a % N_COL
    owner = jnp.where(device_a == device_b, device_a, jnp.where(to_first, cell_a, cell_b))
    ranks = jax.random.permutation(jax.random.fold_in(key, 14), TILES).astype(jnp.int32)
    order = jnp.argsort(owner * TILES + ranks)
    return jnp.stack([first[order], second[order]], axis=1)


def setup_inputs(seed: int = 0) -> dict:
    seeds = jax.random.split(jax.random.key(seed), 5)
    states = draw_states(jax.random.fold_in(seeds[4], 71), 0)
    pool = draw_pool(jax.random.fold_in(seeds[4], 71), 0)
    pick = draw_pick(jax.random.fold_in(seeds[4], 71), 0)
    tile_table = draw_tile_table(jax.random.fold_in(seeds[4], 71), 0)
    return dict(states=states, pool=pool, pick=pick, tile_table=tile_table)


def reference(states, pool, pick, tile_table):
    centres = jnp.take(pool, pick, axis=0)
    inner_part = jnp.dot(states, centres.T, precision=lax.Precision.HIGHEST, preferred_element_type=jnp.float32)
    distance = lax.optimization_barrier(jnp.sum(states * states, axis=1))[:, None] + lax.optimization_barrier(jnp.sum(centres * centres, axis=1))[None, :] - 2.0 * inner_part
    kernel = jnp.exp((2.0 * F - distance) / (4.0 * math.sqrt(F))).astype(jnp.bfloat16)
    panel_blocks = kernel.reshape(SAMPLES, BLOCKS, MB)
    tile_groups = tile_table.reshape(TILES // 64, 64, 2)

    def products(tile_pairs):
        left_blocks = jnp.take(panel_blocks, tile_pairs[:, 0], axis=1).astype(jnp.float32)
        right_blocks = jnp.take(panel_blocks, tile_pairs[:, 1], axis=1).astype(jnp.float32)
        return jnp.einsum('sga,sgb->gab', left_blocks, right_blocks) / SAMPLES
    return lax.map(products, tile_groups).reshape(TILES, MB, MB)
```

```python
import functools
import math

import jax
import jax.numpy as jnp
from jax import lax
from jax.experimental import pallas as pl
from jax.experimental.pallas import tpu as pltpu
from jax.sharding import PartitionSpec as P

F = 1024
M = 16384
MB = 128
N_SA = 4
N_ROW = 4
N_COL = 16
QUART = MB // N_SA


def products_kernel(where_ref, table_ref, r_ref, c_ref, o_ref, g1, g2, rq, cq, *, samples):
    step = pl.program_id(0)
    quarter, row, col = where_ref[0], where_ref[1], where_ref[2]
    nt = (((1,), (1,)), ((), ()))

    @pl.when(step == 0)
    def _():
        g1[...] = jnp.zeros_like(g1)
        g2[...] = jnp.zeros_like(g2)

    def rows(half):
        return pl.ds(pl.multiple_of(half * MB + quarter * QUART, QUART), QUART)

    for dev in range(N_COL):
        for half in range(2):
            rq[(dev * 2 + half) * QUART:(dev * 2 + half + 1) * QUART, :] = r_ref[0, dev, rows(half), :]
    for dev in range(N_ROW):
        for half in range(2):
            cq[(dev * 2 + half) * QUART:(dev * 2 + half + 1) * QUART, :] = c_ref[0, dev, rows(half), :]

    @pl.loop(0, 4)
    def _(m):
        top = pl.ds(pl.multiple_of(m * 256, 256), 256)
        for dev in range(N_ROW):
            got = lax.dot_general(rq[top, :], c_ref[0, dev], nt, preferred_element_type=jnp.float32)
            for half in range(2):
                g1[dev * 2 + half, top, :] += got[:, half * MB:(half + 1) * MB]

    @pl.loop(0, N_COL)
    def _(dev):
        got = lax.dot_general(cq[...], r_ref[0, dev], nt, preferred_element_type=jnp.float32)
        for half in range(2):
            g2[dev * 2 + half, :, :] += got[:, half * MB:(half + 1) * MB]

    @pl.when(step == pl.num_programs(0) - 1)
    def _():
        @pl.loop(0, o_ref.shape[0])
        def _(k):
            i, j = table_ref[0, k], table_ref[1, k]
            row_i, col_i, half_i = i // (2 * N_COL), (i // 2) % N_COL, i % 2
            row_j, col_j, half_j = j // (2 * N_COL), (j // 2) % N_COL, j % 2
            straight = jnp.logical_and(row_i == row, col_j == col)

            @pl.when(straight)
            def _():
                top = pl.ds(pl.multiple_of((col_i * 2 + half_i) * QUART, QUART), QUART)
                o_ref[k] = g1[row_j * 2 + half_j, top, :] / samples

            @pl.when(jnp.logical_not(straight))
            def _():
                top = pl.ds(pl.multiple_of((row_i * 2 + half_i) * QUART, QUART), QUART)
                o_ref[k] = g2[col_j * 2 + half_j, top, :] / samples


def tile_products(where, table, r_all, c_all):
    steps, _, cent, count = r_all.shape
    tiles = table.shape[1]
    return pl.pallas_call(
        functools.partial(products_kernel, samples=float(steps * count)),
        out_shape=jax.ShapeDtypeStruct((tiles, QUART, MB), jnp.float32),
        grid_spec=pltpu.PrefetchScalarGridSpec(
            num_scalar_prefetch=2,
            grid=(steps,),
            in_specs=[
                pl.BlockSpec((1, N_COL, cent, count), lambda q, *_: (q, 0, 0, 0)),
                pl.BlockSpec((1, N_ROW, cent, count), lambda q, *_: (q, 0, 0, 0)),
            ],
            out_specs=pl.BlockSpec((tiles, QUART, MB), lambda q, *_: (0, 0, 0)),
            scratch_shapes=[
                pltpu.VMEM((2 * N_ROW, 2 * N_COL * QUART, MB), jnp.float32),
                pltpu.VMEM((2 * N_COL, 2 * N_ROW * QUART, MB), jnp.float32),
                pltpu.VMEM((2 * N_COL * QUART, count), jnp.bfloat16),
                pltpu.VMEM((2 * N_ROW * QUART, count), jnp.bfloat16),
            ],
        ),
        compiler_params=pltpu.CompilerParams(
            dimension_semantics=("arbitrary",), vmem_limit_bytes=48 * 2**20
        ),
    )(where, table, r_all, c_all)


def partial_distance(states, centres):
    parts = states.reshape(N_SA, states.shape[0] // N_SA, states.shape[1])
    inner = jnp.einsum(
        "cf,qsf->qcs", centres, parts, precision=lax.Precision.HIGHEST, preferred_element_type=jnp.float32
    )
    sample_norms = jnp.sum(parts * parts, axis=2)[:, None, :]
    centre_norms = jnp.sum(centres * centres, axis=1)[None, :, None]
    return sample_norms + centre_norms - 2.0 * inner


def shards(states, pool, pick, tile_table):
    quarter, row, col = lax.axis_index("sa"), lax.axis_index("row"), lax.axis_index("col")
    local = pick - (row * N_COL + col) * pool.shape[0]
    centres = pool.at[local].get(mode="promise_in_bounds")
    distance = lax.psum_scatter(partial_distance(states, centres), "sa", scatter_dimension=0, tiled=False)
    kernel = jnp.exp((2.0 * F - distance) / (4.0 * math.sqrt(F))).astype(jnp.bfloat16)
    cent, count = kernel.shape
    r_all = lax.all_gather(kernel, ("sa", "col")).reshape(N_SA, N_COL, cent, count)
    c_all = lax.all_gather(kernel, ("sa", "row")).reshape(N_SA, N_ROW, cent, count)
    where = jnp.stack([quarter, row, col]).astype(jnp.int32)
    return tile_products(where, tile_table.T, r_all, c_all)


def solution(mesh):
    placed = (P(None, "sa"), P(("row", "col"), "sa"), P(("row", "col")), P(("row", "col"), None))
    return jax.shard_map(
        shards, mesh=mesh, in_specs=placed, out_specs=P(("row", "col"), "sa", None), check_vma=False
    )
```

```python
import functools
import heapq
import math

import jax
import jax.numpy as jnp
from jax import lax
from jax.experimental import pallas as pl
from jax.experimental.pallas import tpu as pltpu
from jax.sharding import PartitionSpec as P

F = 1024
M = 16384
MB = 128
N_SA = 4
N_ROW = 4
N_COL = 16
N_Z = 8
QUART = MB // N_SA
CENT = 256
COUNT = 640
SPLIT = 384
ALL_ROWS = (0, CENT)
LOW_ROWS = (0, CENT // 2)
HIGH_ROWS = (CENT // 2, CENT)
ALL_COLS = (0, COUNT)
Z_FIRST = (0, SPLIT)
Y_FIRST = (SPLIT, COUNT)


class Send:
    def __init__(self, link, src, dst, rows, cols, deps, rank):
        self.link, self.src, self.dst, self.rows, self.cols = link, src, dst, rows, cols
        self.deps, self.rank = deps, rank

    def size(self):
        return 2 * (self.rows[1] - self.rows[0]) * (self.cols[1] - self.cols[0])


def spread_plan():
    sends = []

    def add(*args):
        sends.append(Send(*args))
        return len(sends) - 1

    def ring(axis, size, slot_of, start, cols, deps, rank):
        filled = {}
        for sign, half in (("+", LOW_ROWS), ("-", HIGH_ROWS)):
            step = -1 if sign == "+" else 1
            need, at = deps, start
            for hop in range(1, size // 2 + 1):
                rows = half if hop == size // 2 else ALL_ROWS
                to = (at + step) % size
                k = add(axis + sign, slot_of(at), slot_of(to), rows, cols, need, rank + hop)
                filled.setdefault(to, []).append(k)
                need, at = [k], to
        return filled

    y_own = ring("y", N_SA, lambda d: ("R", d, 0, 0), 0, ALL_COLS, [], 0)
    z_own = ring("z", N_Z, lambda d: ("R", 0, d, 0), 0, Z_FIRST, [], 0)
    arrived = {}
    for dz in range(1, N_Z):
        arrived[0, dz, Z_FIRST] = z_own[dz]
        got = ring("y", N_SA, lambda d: ("R", d, dz, 0), 0, Z_FIRST, z_own[dz], 10)
        for dy in range(1, N_SA):
            arrived[dy, dz, Z_FIRST] = got[dy]
    for dy in range(N_SA):
        need = y_own[dy] if dy else []
        got = ring("z", N_Z, lambda d: ("R", dy, d, 0), 0, Y_FIRST, need, 10)
        for dz in range(1, N_Z):
            arrived[dy, dz, Y_FIRST] = got[dz]
        ring("x", N_ROW, lambda d: ("C", dy, d) if d else ("R", dy, 0, 0), 0, ALL_COLS, need, 20)
        add("s", ("R", dy, 0, 0), ("R", dy, 0, 1), ALL_ROWS, ALL_COLS, need, 30)
    for (dy, dz, cols), need in arrived.items():
        add("s", ("R", dy, dz, 0), ("R", dy, dz, 1), ALL_ROWS, cols, need, 30)
    return sends


def spread_order(sends):
    rate = {"s": 200e3}
    free, pending, done, events, queue = {}, set(range(len(sends))), set(), [], []

    def start_ready(now):
        ready = sorted((k for k in pending if all(d in done for d in sends[k].deps)), key=lambda k: (sends[k].rank, k))
        for k in ready:
            pending.discard(k)
            link = sends[k].link
            begin = max(now, free.get(link, 0.0))
            free[link] = begin + sends[k].size() / rate.get(link, 46e3)
            heapq.heappush(queue, (free[link] + 1.7, k))
        return ready

    events.append((None, start_ready(0.0)))
    while queue:
        now, k = heapq.heappop(queue)
        done.add(k)
        events.append((k, start_ready(now)))
    return events, max(free.values())


def spread_kernel(sends, events, part, r_out, c_out, from_low, from_high, merge, kernel_own, rs_send, rs_recv, out_sems,
                  in_sems, own_sem):
    y, x, col = lax.axis_index("sa"), lax.axis_index("row"), lax.axis_index("col")
    z, core = col // 2, col % 2
    yp, yo, ym = (y + 1) % N_SA, (y + 2) % N_SA, (y + 3) % N_SA
    to = {
        "y+": {"sa": yp},
        "y-": {"sa": ym},
        "x+": {"row": (x + 1) % N_ROW},
        "x-": {"row": (x + 3) % N_ROW},
        "z+": {"col": (z + 1) % N_Z * 2 + core},
        "z-": {"col": (z + 7) % N_Z * 2 + core},
        "s": {"col": z * 2 + 1 - core},
    }
    mesh_id = pl.DeviceIdType.MESH
    barrier = pltpu.get_barrier_semaphore()
    for peer in to.values():
        pl.semaphore_signal(barrier, inc=1, device_id=peer, device_id_type=mesh_id)
    pl.semaphore_wait(barrier, len(to))

    low, high = pl.ds(0, CENT // 2), pl.ds(CENT // 2, CENT // 2)

    def rs(src, buf, slot, link):
        way = 0 if link == "y+" else 3
        copy = pltpu.make_async_remote_copy(
            src_ref=src, dst_ref=buf.at[slot], send_sem=rs_send.at[way + slot], recv_sem=rs_recv.at[way + slot],
            device_id=to[link], device_id_type=mesh_id)
        copy.start()
        return copy

    copies = [
        rs(part.at[yo, low], from_low, 0, "y+"),
        rs(part.at[yo, high], from_high, 0, "y-"),
        rs(part.at[yp, high], from_low, 1, "y+"),
        rs(part.at[ym, low], from_high, 1, "y-"),
    ]
    copies[0].wait_recv()
    merge[0] = part[yp, :CENT // 2] + from_low[0]
    copies.append(rs(merge.at[0], from_low, 2, "y+"))
    copies[1].wait_recv()
    merge[1] = part[ym, CENT // 2:] + from_high[0]
    copies.append(rs(merge.at[1], from_high, 2, "y-"))
    for k in range(2, 6):
        copies[k].wait_recv()
    low_sum = part[y, :CENT // 2] + from_low[2] + from_high[1]
    kernel_own[:CENT // 2] = jnp.exp((2.0 * F - low_sum) / (4.0 * math.sqrt(F))).astype(jnp.bfloat16)
    high_sum = part[y, CENT // 2:] + from_low[1] + from_high[2]
    kernel_own[CENT // 2:] = jnp.exp((2.0 * F - high_sum) / (4.0 * math.sqrt(F))).astype(jnp.bfloat16)
    for copy in copies:
        copy.wait_send()

    own = pltpu.make_async_copy(kernel_own, r_out.at[0, 0], own_sem)
    own.start()

    def slot(place, rows, cols, source):
        rows, cols = pl.ds(rows[0], rows[1] - rows[0]), pl.ds(cols[0], cols[1] - cols[0])
        if source and place == ("R", 0, 0, 0):
            return kernel_own.at[rows, cols]
        if place[0] == "R":
            return r_out.at[place[1], place[2] * 2 + place[3], rows, cols]
        return c_out.at[place[1], place[2] - 1, rows, cols]

    started = {}
    for k, send in enumerate(sends):
        started[k] = pltpu.make_async_remote_copy(
            src_ref=slot(send.src, send.rows, send.cols, True), dst_ref=slot(send.dst, send.rows, send.cols, False),
            send_sem=out_sems.at[k], recv_sem=in_sems.at[k], device_id=to[send.link], device_id_type=mesh_id)
    for arrival, ready in events:
        if arrival is not None:
            started[arrival].wait_recv()
        for k in ready:
            started[k].start()
    own.wait()
    for copy in started.values():
        copy.wait_send()


def spread(part):
    sends = spread_plan()
    events, _ = spread_order(sends)
    half = (CENT // 2, COUNT)
    anywhere = pl.BlockSpec(memory_space=pl.ANY)
    return pl.pallas_call(
        functools.partial(spread_kernel, sends, events),
        out_shape=(
            jax.ShapeDtypeStruct((N_SA, N_COL, CENT, COUNT), jnp.bfloat16),
            jax.ShapeDtypeStruct((N_SA, N_ROW - 1, CENT, COUNT), jnp.bfloat16),
        ),
        in_specs=[pl.BlockSpec(memory_space=pltpu.VMEM)],
        out_specs=(anywhere, anywhere),
        scratch_shapes=[
            pltpu.VMEM((3, *half), jnp.float32),
            pltpu.VMEM((3, *half), jnp.float32),
            pltpu.VMEM((2, *half), jnp.float32),
            pltpu.VMEM((CENT, COUNT), jnp.bfloat16),
            pltpu.SemaphoreType.DMA((6,)),
            pltpu.SemaphoreType.DMA((6,)),
            pltpu.SemaphoreType.DMA((len(sends),)),
            pltpu.SemaphoreType.DMA((len(sends),)),
            pltpu.SemaphoreType.DMA,
        ],
        compiler_params=pltpu.CompilerParams(
            collective_id=0, has_side_effects=True, vmem_limit_bytes=24 * 2**20
        ),
    )(part)


def products_kernel(where_ref, table_ref, r_ref, c_ref, o_ref, g1, g2, rq, cq, *, samples):
    step = pl.program_id(0)
    quarter, row, col = where_ref[0], where_ref[1], where_ref[2]
    nt = (((1,), (1,)), ((), ()))

    @pl.when(step == 0)
    def _():
        g1[...] = jnp.zeros_like(g1)
        g2[...] = jnp.zeros_like(g2)

    def rows(half):
        return pl.ds(pl.multiple_of(half * MB + quarter * QUART, QUART), QUART)

    def column(dev):
        return c_ref.at[0, dev - 1] if dev else r_ref.at[0, 0]

    for dev in range(N_COL):
        for half in range(2):
            rq[(dev * 2 + half) * QUART:(dev * 2 + half + 1) * QUART, :] = r_ref[0, dev, rows(half), :]
    for dev in range(N_ROW):
        for half in range(2):
            cq[(dev * 2 + half) * QUART:(dev * 2 + half + 1) * QUART, :] = column(dev)[rows(half), :]

    @pl.loop(0, 4)
    def _(m):
        top = pl.ds(pl.multiple_of(m * 256, 256), 256)
        for dev in range(N_ROW):
            got = lax.dot_general(rq[top, :], column(dev)[...], nt, preferred_element_type=jnp.float32)
            for half in range(2):
                g1[dev * 2 + half, top, :] += got[:, half * MB:(half + 1) * MB]

    @pl.loop(0, N_COL)
    def _(dev):
        got = lax.dot_general(cq[...], r_ref[0, dev], nt, preferred_element_type=jnp.float32)
        for half in range(2):
            g2[dev * 2 + half, :, :] += got[:, half * MB:(half + 1) * MB]

    @pl.when(step == pl.num_programs(0) - 1)
    def _():
        @pl.loop(0, o_ref.shape[0])
        def _(k):
            i, j = table_ref[0, k], table_ref[1, k]
            row_i, col_i, half_i = i // (2 * N_COL), (i // 2) % N_COL, i % 2
            row_j, col_j, half_j = j // (2 * N_COL), (j // 2) % N_COL, j % 2
            straight = jnp.logical_and(row_i == row, col_j == col)

            def far_col(c):
                return (c // 2 - col // 2 + N_Z) % N_Z * 2 + (c + col) % 2

            def far_row(r):
                return (r - row + N_ROW) % N_ROW

            @pl.when(straight)
            def _():
                top = pl.ds(pl.multiple_of((far_col(col_i) * 2 + half_i) * QUART, QUART), QUART)
                o_ref[k] = g1[far_row(row_j) * 2 + half_j, top, :] / samples

            @pl.when(jnp.logical_not(straight))
            def _():
                top = pl.ds(pl.multiple_of((far_row(row_i) * 2 + half_i) * QUART, QUART), QUART)
                o_ref[k] = g2[far_col(col_j) * 2 + half_j, top, :] / samples


def tile_products(where, table, r_all, c_all):
    steps, _, cent, count = r_all.shape
    tiles = table.shape[1]
    return pl.pallas_call(
        functools.partial(products_kernel, samples=float(steps * count)),
        out_shape=jax.ShapeDtypeStruct((tiles, QUART, MB), jnp.float32),
        grid_spec=pltpu.PrefetchScalarGridSpec(
            num_scalar_prefetch=2,
            grid=(steps,),
            in_specs=[
                pl.BlockSpec((1, N_COL, cent, count), lambda q, *_: (q, 0, 0, 0)),
                pl.BlockSpec((1, N_ROW - 1, cent, count), lambda q, *_: (q, 0, 0, 0)),
            ],
            out_specs=pl.BlockSpec((tiles, QUART, MB), lambda q, *_: (0, 0, 0)),
            scratch_shapes=[
                pltpu.VMEM((2 * N_ROW, 2 * N_COL * QUART, MB), jnp.float32),
                pltpu.VMEM((2 * N_COL, 2 * N_ROW * QUART, MB), jnp.float32),
                pltpu.VMEM((2 * N_COL * QUART, count), jnp.bfloat16),
                pltpu.VMEM((2 * N_ROW * QUART, count), jnp.bfloat16),
            ],
        ),
        compiler_params=pltpu.CompilerParams(
            dimension_semantics=("arbitrary",), vmem_limit_bytes=48 * 2**20
        ),
    )(where, table, r_all, c_all)


def partial_distance(states, centres):
    parts = states.reshape(N_SA, states.shape[0] // N_SA, states.shape[1])
    inner = jnp.einsum(
        "cf,qsf->qcs", centres, parts, precision=lax.Precision.HIGHEST, preferred_element_type=jnp.float32
    )
    sample_norms = jnp.sum(parts * parts, axis=2)[:, None, :]
    centre_norms = jnp.sum(centres * centres, axis=1)[None, :, None]
    return sample_norms + centre_norms - 2.0 * inner


def shards(states, pool, pick, tile_table):
    quarter, row, col = lax.axis_index("sa"), lax.axis_index("row"), lax.axis_index("col")
    local = pick - (row * N_COL + col) * pool.shape[0]
    centres = pool.at[local].get(mode="promise_in_bounds")
    r_all, c_all = spread(partial_distance(states, centres))
    where = jnp.stack([quarter, row, col]).astype(jnp.int32)
    return tile_products(where, tile_table.T, r_all, c_all)


def solution(mesh):
    placed = (P(None, "sa"), P(("row", "col"), "sa"), P(("row", "col")), P(("row", "col"), None))
    return jax.shard_map(
        shards, mesh=mesh, in_specs=placed, out_specs=P(("row", "col"), "sa", None), check_vma=False
    )
```

```python
import functools
import heapq
import math

import jax
import jax.numpy as jnp
from jax import lax
from jax.experimental import pallas as pl
from jax.experimental.pallas import tpu as pltpu
from jax.sharding import PartitionSpec as P

F = 1024
M = 16384
MB = 128
N_SA = 4
N_ROW = 4
N_COL = 16
N_Z = 8
QUART = MB // N_SA
CENT = 256
COUNT = 640
SPLIT = 384
ALL_ROWS = (0, CENT)
LOW_ROWS = (0, CENT // 2)
HIGH_ROWS = (CENT // 2, CENT)
ALL_COLS = (0, COUNT)
Z_FIRST = (0, SPLIT)
Y_FIRST = (SPLIT, COUNT)


class Send:
    def __init__(self, link, src, dst, rows, cols, deps, rank):
        self.link, self.src, self.dst, self.rows, self.cols = link, src, dst, rows, cols
        self.deps, self.rank = deps, rank

    def size(self):
        return 2 * (self.rows[1] - self.rows[0]) * (self.cols[1] - self.cols[0])


def spread_plan():
    sends = []

    def add(*args):
        sends.append(Send(*args))
        return len(sends) - 1

    def ring(axis, size, slot_of, start, cols, deps, rank):
        filled = {}
        for sign, half in (("+", LOW_ROWS), ("-", HIGH_ROWS)):
            step = -1 if sign == "+" else 1
            need, at = deps, start
            for hop in range(1, size // 2 + 1):
                rows = half if hop == size // 2 else ALL_ROWS
                to = (at + step) % size
                k = add(axis + sign, slot_of(at), slot_of(to), rows, cols, need, rank + hop)
                filled.setdefault(to, []).append(k)
                need, at = [k], to
        return filled

    y_own = ring("y", N_SA, lambda d: ("R", d, 0, 0), 0, ALL_COLS, [], 0)
    z_own = ring("z", N_Z, lambda d: ("R", 0, d, 0), 0, Z_FIRST, [], 0)
    arrived = {}
    for dz in range(1, N_Z):
        arrived[0, dz, Z_FIRST] = z_own[dz]
        got = ring("y", N_SA, lambda d: ("R", d, dz, 0), 0, Z_FIRST, z_own[dz], 10)
        for dy in range(1, N_SA):
            arrived[dy, dz, Z_FIRST] = got[dy]
    for dy in range(N_SA):
        need = y_own[dy] if dy else []
        got = ring("z", N_Z, lambda d: ("R", dy, d, 0), 0, Y_FIRST, need, 10)
        for dz in range(1, N_Z):
            arrived[dy, dz, Y_FIRST] = got[dz]
        ring("x", N_ROW, lambda d: ("C", dy, d) if d else ("R", dy, 0, 0), 0, ALL_COLS, need, 20)
        add("s", ("R", dy, 0, 0), ("R", dy, 0, 1), ALL_ROWS, ALL_COLS, need, 30)
    for (dy, dz, cols), need in arrived.items():
        add("s", ("R", dy, dz, 0), ("R", dy, dz, 1), ALL_ROWS, cols, need, 30)
    return sends


def spread_order(sends):
    rate = {"s": 200e3}
    free, pending, done, events, queue = {}, set(range(len(sends))), set(), [], []

    def start_ready(now):
        ready = sorted((k for k in pending if all(d in done for d in sends[k].deps)), key=lambda k: (sends[k].rank, k))
        for k in ready:
            pending.discard(k)
            link = sends[k].link
            begin = max(now, free.get(link, 0.0))
            free[link] = begin + sends[k].size() / rate.get(link, 46e3)
            heapq.heappush(queue, (free[link] + 1.7, k))
        return ready

    events.append((None, start_ready(0.0)))
    while queue:
        now, k = heapq.heappop(queue)
        done.add(k)
        events.append((k, start_ready(now)))
    return events, max(free.values())


def slot_of(place):
    return place[2] * 2 + place[3]


def left_place(dev, half, slot, slot_half):
    return (dev * 2 + half) * 2 * N_COL + slot * 2 + slot_half


def right_place(slot, half, place):
    return 2 * N_ROW * 2 * N_COL + (slot * 2 + half) * 2 * N_ROW + place


def table_places(table, x, col):
    i, j = table[:, 0], table[:, 1]
    row_i, col_i, half_i = i // (2 * N_COL), (i // 2) % N_COL, i % 2
    row_j, col_j, half_j = j // (2 * N_COL), (j // 2) % N_COL, j % 2

    def far_col(c):
        return (c // 2 - col // 2 + N_Z) % N_Z * 2 + (c + col) % 2

    def far_row(r):
        return (r - x + N_ROW) % N_ROW

    straight = jnp.logical_and(row_i == x, col_j == col)
    left = left_place(far_row(row_j), half_j, far_col(col_i), half_i)
    right = right_place(far_col(col_j), half_j, far_row(row_i) * 2 + half_i)
    return jnp.where(straight, left, right).astype(jnp.int32)


def compute_plan(sends, events):
    left_r, left_c = {}, 0
    for send in sends:
        if send.dst[0] == "R":
            left_r[slot_of(send.dst)] = left_r.get(slot_of(send.dst), 0) + 1
        else:
            left_c += 1
    ready, group, plan, waiting = [], [], [], []
    for arrival, _ in events:
        if arrival is not None:
            send = sends[arrival]
            if send.dst[0] == "C":
                left_c -= 1
                if left_c == 0:
                    ready.append(("columns", None))
                    ready.extend(waiting)
                    waiting = []
            else:
                slot = slot_of(send.dst)
                left_r[slot] -= 1
                if left_r[slot] == 0:
                    todo = [("right", slot)]
                    group.append(slot)
                    if len(group) == 4:
                        todo.append(("rows", tuple(group)))
                        todo.extend(("left", (tuple(group), dev)) for dev in range(N_ROW))
                        group = []
                    if left_c:
                        waiting.extend(todo)
                    else:
                        ready.extend(todo)
        plan.append([ready.pop(0)] if ready else [])
    plan[-1].extend(ready)
    return plan


def spread_kernel(sends, events, plan, place_of, part, o_ref, r_all, c_all, blocks, rq, cq, from_low, from_high, merge,
                  rs_send, rs_recv, out_sems, in_sems):
    y, x, col = lax.axis_index("sa"), lax.axis_index("row"), lax.axis_index("col")
    z, core = col // 2, col % 2
    yp, yo, ym = (y + 1) % N_SA, (y + 2) % N_SA, (y + 3) % N_SA
    to = {
        "y+": {"sa": yp},
        "y-": {"sa": ym},
        "x+": {"row": (x + 1) % N_ROW},
        "x-": {"row": (x + 3) % N_ROW},
        "z+": {"col": (z + 1) % N_Z * 2 + core},
        "z-": {"col": (z + 7) % N_Z * 2 + core},
        "s": {"col": z * 2 + 1 - core},
    }
    mesh_id = pl.DeviceIdType.MESH
    barrier = pltpu.get_barrier_semaphore()
    for peer in to.values():
        pl.semaphore_signal(barrier, inc=1, device_id=peer, device_id_type=mesh_id)
    pl.semaphore_wait(barrier, len(to))

    low, high = pl.ds(0, CENT // 2), pl.ds(CENT // 2, CENT // 2)

    def rs(src, buf, slot, link):
        way = 0 if link == "y+" else 3
        copy = pltpu.make_async_remote_copy(
            src_ref=src, dst_ref=buf.at[slot], send_sem=rs_send.at[way + slot], recv_sem=rs_recv.at[way + slot],
            device_id=to[link], device_id_type=mesh_id)
        copy.start()
        return copy

    copies = [
        rs(part.at[yo, low], from_low, 0, "y+"),
        rs(part.at[yo, high], from_high, 0, "y-"),
        rs(part.at[yp, high], from_low, 1, "y+"),
        rs(part.at[ym, low], from_high, 1, "y-"),
    ]
    copies[0].wait_recv()
    merge[0] = part[yp, :CENT // 2] + from_low[0]
    copies.append(rs(merge.at[0], from_low, 2, "y+"))
    copies[1].wait_recv()
    merge[1] = part[ym, CENT // 2:] + from_high[0]
    copies.append(rs(merge.at[1], from_high, 2, "y-"))
    for k in range(2, 6):
        copies[k].wait_recv()
    low_sum = part[y, :CENT // 2] + from_low[2] + from_high[1]
    r_all[0, :CENT // 2, :COUNT] = jnp.exp((2.0 * F - low_sum) / (4.0 * math.sqrt(F))).astype(jnp.bfloat16)
    high_sum = part[y, CENT // 2:] + from_low[1] + from_high[2]
    r_all[0, CENT // 2:, :COUNT] = jnp.exp((2.0 * F - high_sum) / (4.0 * math.sqrt(F))).astype(jnp.bfloat16)
    for copy in copies:
        copy.wait_send()

    def place_ref(place, rows, cols):
        rows = pl.ds(rows[0], rows[1] - rows[0])
        cols = pl.ds(place[1] * COUNT + cols[0], cols[1] - cols[0])
        if place[0] == "R":
            return r_all.at[slot_of(place), rows, cols]
        return c_all.at[place[2] - 1, rows, cols]

    def column(dev):
        return c_all.at[dev - 1] if dev else r_all.at[0]

    def quarter(half):
        return pl.ds(pl.multiple_of(half * MB + y * QUART, QUART), QUART)

    def dot(left, right):
        return lax.dot_general(left, right, (((1,), (1,)), ((), ())), preferred_element_type=jnp.float32)

    def compute(kind, what):
        if kind == "columns":
            for dev in range(N_ROW):
                for half in range(2):
                    top = (dev * 2 + half) * QUART
                    cq[top:top + QUART, :] = column(dev)[quarter(half), :]
        elif kind == "rows":
            for n, slot in enumerate(what):
                for half in range(2):
                    top = (n * 2 + half) * QUART
                    rq[top:top + QUART, :] = r_all[slot, quarter(half), :]
        elif kind == "right":
            got = dot(cq[...], r_all[what])
            for half in range(2):
                for n in range(2 * N_ROW):
                    blocks[right_place(what, half, n)] = got[n * QUART:(n + 1) * QUART, half * MB:(half + 1) * MB]
        else:
            slots, dev = what
            got = dot(rq[...], column(dev)[...])
            for half in range(2):
                for n in range(8):
                    blocks[left_place(dev, half, slots[n // 2], n % 2)] = got[
                        n * QUART:(n + 1) * QUART, half * MB:(half + 1) * MB]

    started = []
    for k, send in enumerate(sends):
        started.append(pltpu.make_async_remote_copy(
            src_ref=place_ref(send.src, send.rows, send.cols), dst_ref=place_ref(send.dst, send.rows, send.cols),
            send_sem=out_sems.at[k], recv_sem=in_sems.at[k], device_id=to[send.link], device_id_type=mesh_id))
    for (arrival, ready), tasks in zip(events, plan):
        if arrival is not None:
            started[arrival].wait_recv()
        for k in ready:
            started[k].start()
        for task in tasks:
            compute(*task)
    for copy in started:
        copy.wait_send()

    @pl.loop(0, o_ref.shape[0] // 3)
    def _(step):
        for n in range(3):
            k = step * 3 + n
            o_ref[k] = blocks[place_of[k]] * (1.0 / (N_SA * COUNT))


def spread(place_of, part):
    sends = spread_plan()
    events, _ = spread_order(sends)
    half = (CENT // 2, COUNT)
    whole = N_SA * COUNT
    vmem = pl.BlockSpec(memory_space=pltpu.VMEM)
    return pl.pallas_call(
        functools.partial(spread_kernel, sends, events, compute_plan(sends, events)),
        out_shape=jax.ShapeDtypeStruct((place_of.shape[0], QUART, MB), jnp.float32),
        in_specs=[pl.BlockSpec(memory_space=pltpu.SMEM), vmem],
        out_specs=vmem,
        scratch_shapes=[
            pltpu.VMEM((N_COL, CENT, whole), jnp.bfloat16),
            pltpu.VMEM((N_ROW - 1, CENT, whole), jnp.bfloat16),
            pltpu.VMEM((2 * 2 * N_ROW * 2 * N_COL, QUART, MB), jnp.float32),
            pltpu.VMEM((CENT, whole), jnp.bfloat16),
            pltpu.VMEM((CENT, whole), jnp.bfloat16),
            pltpu.VMEM((3, *half), jnp.float32),
            pltpu.VMEM((3, *half), jnp.float32),
            pltpu.VMEM((2, *half), jnp.float32),
            pltpu.SemaphoreType.DMA((6,)),
            pltpu.SemaphoreType.DMA((6,)),
            pltpu.SemaphoreType.DMA((len(sends),)),
            pltpu.SemaphoreType.DMA((len(sends),)),
        ],
        compiler_params=pltpu.CompilerParams(
            collective_id=0, has_side_effects=True, vmem_limit_bytes=52 * 2**20
        ),
    )(place_of, part)


def partial_distance(states, centres):
    parts = states.reshape(N_SA, states.shape[0] // N_SA, states.shape[1])
    inner = jnp.einsum(
        "cf,qsf->qcs", centres, parts, precision=lax.Precision.HIGHEST, preferred_element_type=jnp.float32
    )
    sample_norms = jnp.sum(parts * parts, axis=2)[:, None, :]
    centre_norms = jnp.sum(centres * centres, axis=1)[None, :, None]
    return sample_norms + centre_norms - 2.0 * inner


def shards(states, pool, pick, tile_table):
    row, col = lax.axis_index("row"), lax.axis_index("col")
    local = pick - (row * N_COL + col) * pool.shape[0]
    centres = pool.at[local].get(mode="promise_in_bounds")
    return spread(table_places(tile_table, row, col), partial_distance(states, centres))


def solution(mesh):
    placed = (P(None, "sa"), P(("row", "col"), "sa"), P(("row", "col")), P(("row", "col"), None))
    return jax.shard_map(
        shards, mesh=mesh, in_specs=placed, out_specs=P(("row", "col"), "sa", None), check_vma=False
    )
```

```python
import functools
import heapq
import math

import jax
import jax.numpy as jnp
from jax import lax
from jax.experimental import pallas as pl
from jax.experimental.pallas import tpu as pltpu
from jax.sharding import PartitionSpec as P

F = 1024
M = 16384
MB = 128
N_SA = 4
N_ROW = 4
N_COL = 16
N_Z = 8
QUART = MB // N_SA
CENT = 256
COUNT = 640
POOL_DEV = 512
FEAT = F // N_SA
SHARE = COUNT // 8
SPLIT = 384
Z_FIRST = (0, SPLIT)
Y_FIRST = (SPLIT, COUNT)
EVERY = (0, COUNT)
GROUPS = ((0, 1, 2, 14), (3, 15, 4, 12), (5, 13, 6, 10), (7, 11, 8, 9))
RATE = {"s": 300e3}
LINK_RATE = 45e3
LATENCY = 1.7


class Send:
    def __init__(self, link, src, dst, size, deps, rank):
        self.link, self.src, self.dst, self.size = link, src, dst, size
        self.deps, self.rank = tuple(deps), rank


def ring(sends, axis, size, unit, own, halves, nbytes, deps, rank):
    filled = {}
    for sign, half in (("+", halves[0]), ("-", halves[1])):
        step = -1 if sign == "+" else 1
        need, at = deps, 0
        for hop in range(1, size // 2 + 1):
            last = hop == size // 2
            part = half if last else None
            to = (at + step) % size
            src = own(part) if at == 0 else unit(at, part)
            sends.append(Send(axis + sign, src, unit(to, part), nbytes // 2 if last else nbytes, need, rank + hop))
            filled.setdefault(to, []).append(len(sends) - 1)
            need, at = [len(sends) - 1], to
    return filled


def gather_inputs_plan():
    sends, tasks = [], []
    row_bytes = 4 * FEAT
    half = SHARE // 2

    def add(*args):
        sends.append(Send(*args))
        return len(sends) - 1

    relay = [add("y+", ("H", 2, 0, half), ("B", 0), half * row_bytes, (), 0),
             add("y-", ("H", 2, half, half), ("B", 1), half * row_bytes, (), 0)]
    come = {3: [add("y+", ("H", 1, 0, SHARE), ("S", 3, 0, 0, 0, SHARE), SHARE * row_bytes, (), 1)],
            1: [add("y-", ("H", 3, 0, SHARE), ("S", 1, 0, 0, 0, SHARE), SHARE * row_bytes, (), 1)]}
    come[2] = [add("y+", ("B", 0), ("S", 2, 0, 0, 0, half), half * row_bytes, relay[:1], 0),
               add("y-", ("B", 1), ("S", 2, 0, 0, half, half), half * row_bytes, relay[1:], 0)]

    def rows(part):
        return (0, SHARE) if part is None else part

    states = {}
    for d in (3, 1, 2):
        got = ring(sends, "x", N_ROW, lambda dx, part: ("S", d, dx, 0, *rows(part)),
                   lambda part: ("S", d, 0, 0, *rows(part)), ((0, half), (half, half)), SHARE * row_bytes, come[d], 0)
        got[0] = come[d]
        states[d] = [k for dx in range(N_ROW) for k in got[dx]]
        for dx in (0, 3, 1, 2):
            k = add("s", ("S", d, dx, 0, 0, SHARE), ("S", d, dx, 0, 0, SHARE), SHARE * row_bytes, got[dx], 5)
            states[d].append(k)

    def cent(part):
        return (0, CENT) if part is None else part

    halves = ((0, CENT // 2), (CENT // 2, CENT // 2))
    centres = ring(sends, "y", N_SA, lambda d, part: ("F", d, *cent(part)), lambda part: ("F", 0, *cent(part)), halves,
                   CENT * row_bytes, ("local", *relay), 3)
    tasks.append((("distance", 0), ("local",), 0.8))
    for d in (3, 1, 2):
        tasks.append((("distance", d), tuple(states[d] + centres[d]), 0.8))
    return sends, tasks


def spread_plan():
    sends = []

    def cut(cols, half):
        first, rows = (0, CENT) if half is None else half
        return (first, rows, cols[0], cols[1] - cols[0])

    halves = ((0, CENT // 2), (CENT // 2, CENT // 2))

    def area(cols):
        return 2 * CENT * (cols[1] - cols[0])

    def r_ring(axis, size, place, cols, deps, rank):
        return ring(sends, axis, size, lambda d, half: ("R", *place(d), 0, cut(cols, half)),
                    lambda half: ("R", *place(0), 0, cut(cols, half)), halves, area(cols), deps, rank)

    y_own = r_ring("y", N_SA, lambda d: (d, 0), EVERY, (), 0)
    z_own = r_ring("z", N_Z, lambda d: (0, d), Z_FIRST, (), 0)
    arrived = {}
    for dz in range(1, N_Z):
        arrived[0, dz, Z_FIRST] = z_own[dz]
        got = r_ring("y", N_SA, lambda d: (d, dz), Z_FIRST, z_own[dz], 10)
        for dy in range(1, N_SA):
            arrived[dy, dz, Z_FIRST] = got[dy]
    in_r, in_c = {(dy, 0): list(y_own[dy]) if dy else [] for dy in range(N_SA)}, {}
    for dy in range(N_SA):
        need = in_r[dy, 0]
        got = r_ring("z", N_Z, lambda d: (dy, d), Y_FIRST, need, 10)
        for dz in range(1, N_Z):
            arrived[dy, dz, Y_FIRST] = got[dz]
        got = ring(sends, "x", N_ROW, lambda d, half: ("C", dy, d, cut(EVERY, half)),
                   lambda half: ("R", dy, 0, 0, cut(EVERY, half)), halves, area(EVERY), need, 20)
        in_c[dy] = [k for ks in got.values() for k in ks] + need
        sends.append(Send("s", ("R", dy, 0, 0, cut(EVERY, None)), ("R", dy, 0, 1, cut(EVERY, None)), area(EVERY), need, 30))
        in_r[dy, 1] = [len(sends) - 1]
    for (dy, dz, cols), need in arrived.items():
        sends.append(Send("s", ("R", dy, dz, 0, cut(cols, None)), ("R", dy, dz, 1, cut(cols, None)), area(cols), need, 30))
        in_r.setdefault((dy, dz * 2), []).extend(need)
        in_r.setdefault((dy, dz * 2 + 1), []).append(len(sends) - 1)

    tasks = []
    for dy in range(N_SA):
        tasks.append((("columns", dy), tuple(in_c[dy]), 0.15))
    for group in GROUPS:
        for dy in range(N_SA):
            need = [k for slot in group for k in in_r[dy, slot]] + in_c[dy]
            tasks.append((("right", (group, dy)), tuple(need), 0.5))
            tasks.append((("left", (group, dy)), tuple(need), 0.5))
    return sends, tasks


def timetable(sends, tasks, local):
    free, pending, done, queue, steps = {}, set(range(len(sends))), set(), [], []
    undone = list(range(len(tasks)))

    def start_ready(now):
        ready = sorted((k for k in pending if all(d in done for d in sends[k].deps)), key=lambda k: (sends[k].rank, k))
        for k in ready:
            pending.discard(k)
            link = sends[k].link
            free[link] = max(now, free.get(link, 0.0)) + sends[k].size / RATE.get(link, LINK_RATE)
            heapq.heappush(queue, (free[link] + LATENCY, k))
            steps.append(("start", k))

    core = 0.0
    start_ready(core)
    if local is not None:
        core += local
        steps.append(("local", None))
        done.add("local")
        start_ready(core)
    while queue or undone:
        coming = queue[0][0] if queue else math.inf
        ready = [t for t in undone if all(d in done for d in tasks[t][1])]
        if ready and coming - core >= 0.6 * tasks[ready[0]][2]:
            undone.remove(ready[0])
            core += tasks[ready[0]][2]
            steps.append(("task", tasks[ready[0]][0]))
            continue
        now, k = heapq.heappop(queue)
        core = max(core, now)
        done.add(k)
        steps.append(("wait", k))
        start_ready(core)
    return steps, core


def left_place(dev, half, slot, slot_half):
    return (dev * 2 + half) * 2 * N_COL + slot * 2 + slot_half


def right_place(slot, half, place):
    return 2 * N_ROW * 2 * N_COL + (slot * 2 + half) * 2 * N_ROW + place


def normal_kernel(plans, steps, table, pick, states, pool, o_ref, r_all, c_all, blocks, cq, rq, s_all, f_all, relay,
                  pool_local, inner, sample_norms, centre_norms, place_of, copy_sems, first_out, first_in, out_sems,
                  in_sems):
    y, x, col = lax.axis_index("sa"), lax.axis_index("row"), lax.axis_index("col")
    z, core = col // 2, col % 2
    to = {
        "y+": {"sa": (y + 1) % N_SA},
        "y-": {"sa": (y + 3) % N_SA},
        "x+": {"row": (x + 1) % N_ROW},
        "x-": {"row": (x + 3) % N_ROW},
        "z+": {"col": (z + 1) % N_Z * 2 + core},
        "z-": {"col": (z + 7) % N_Z * 2 + core},
        "s": {"col": z * 2 + 1 - core},
    }
    mesh_id = pl.DeviceIdType.MESH
    pool_copy = pltpu.make_async_copy(pool, pool_local, copy_sems.at[0])
    pool_copy.start()
    states_copy = pltpu.make_async_copy(
        states.at[pl.ds(pl.multiple_of(y * COUNT, COUNT), COUNT), :], s_all.at[0], copy_sems.at[1])
    states_copy.start()
    barrier = pltpu.get_barrier_semaphore()
    for peer in to.values():
        pl.semaphore_signal(barrier, inc=1, device_id=peer, device_id_type=mesh_id)
    pl.semaphore_wait(barrier, len(to))

    def place_ref(place):
        kind = place[0]
        if kind == "H":
            first = (y + place[1]) % N_SA * COUNT + (x * 2 + core) * SHARE + place[2]
            return states.at[pl.ds(pl.multiple_of(first, 8), place[3]), :]
        if kind == "B":
            return relay.at[place[1]]
        if kind == "S":
            first = ((x + place[2]) % N_ROW * 2 + core) * SHARE + place[4]
            return s_all.at[place[1], pl.ds(pl.multiple_of(first, 8), place[5]), :]
        if kind == "F":
            return f_all.at[place[1], pl.ds(place[2], place[3]), :]
        first, rows, start, count = place[-1]
        rows, cols = pl.ds(first, rows), pl.ds(place[1] * COUNT + start, count)
        if kind == "R":
            return r_all.at[place[2] * 2 + place[3], rows, cols]
        return c_all.at[place[2] - 1, rows, cols]

    def landing(send):
        if send.src[0] == "S":
            return place_ref(send.src)
        return place_ref(send.dst)

    def copies_of(sends, out, into):
        return [
            pltpu.make_async_remote_copy(
                src_ref=place_ref(send.src), dst_ref=landing(send), send_sem=out.at[k], recv_sem=into.at[k],
                device_id=to[send.link], device_id_type=mesh_id)
            for k, send in enumerate(sends)
        ]

    def dot(left, right, precision=None):
        return lax.dot_general(left, right, (((1,), (1,)), ((), ())), precision=precision,
                               preferred_element_type=jnp.float32)

    def distance(d):
        sample, centre = s_all[d], f_all[d]
        cross = dot(centre, sample, lax.Precision.HIGHEST)
        norms = dot(jnp.ones((8, FEAT), jnp.float32), sample * sample, lax.Precision.HIGHEST)
        own = jnp.sum(centre * centre, axis=1, keepdims=True)
        if d:
            inner[...] += cross
            sample_norms[...] += norms
            centre_norms[...] += own
        else:
            inner[...], sample_norms[...], centre_norms[...] = cross, norms, own

    def local():
        pool_copy.wait()

        @pl.loop(0, CENT // 8)
        def _(m):
            for n in range(8):
                f_all[0, m * 8 + n] = pool_local[pick[m * 8 + n] & (POOL_DEV - 1)]

        states_copy.wait()

    def column(dev):
        return c_all.at[dev - 1] if dev else r_all.at[0]

    def quarter(half):
        return pl.ds(pl.multiple_of(half * MB + y * QUART, QUART), QUART)

    begun = set()

    def put(where, value, key):
        if key in begun:
            blocks[where] += value
        else:
            blocks[where] = value

    def task(kind, what):
        if kind == "distance":
            distance(what)
            return
        if kind == "columns":
            cols = slice(what * COUNT, (what + 1) * COUNT)
            for dev in range(N_ROW):
                for half in range(2):
                    top = (dev * 2 + half) * QUART
                    cq[top:top + QUART, cols] = column(dev)[quarter(half), cols]
            return
        group, dy = what
        cols = slice(dy * COUNT, (dy + 1) * COUNT)
        if kind == "right":
            for slot in group:
                got = dot(cq[:, cols], r_all[slot, :, cols])
                for half in range(2):
                    for n in range(2 * N_ROW):
                        put(right_place(slot, half, n), got[n * QUART:(n + 1) * QUART, half * MB:(half + 1) * MB],
                            (kind, group))
        else:
            for n, slot in enumerate(group):
                for half in range(2):
                    top = (n * 2 + half) * QUART
                    rq[top:top + QUART, :] = r_all[slot, quarter(half), cols]
            for dev in range(N_ROW):
                got = dot(rq[...], column(dev)[:, cols])
                for half in range(2):
                    for n in range(8):
                        put(left_place(dev, half, group[n // 2], n % 2),
                            got[n * QUART:(n + 1) * QUART, half * MB:(half + 1) * MB], (kind, group))
        begun.add((kind, group))

    def run(copies, order):
        for kind, what in order:
            if kind == "wait":
                copies[what].wait_recv()
            elif kind == "start":
                copies[what].start()
            elif kind == "local":
                local()
            else:
                task(*what)

    first = copies_of(plans[0], first_out, first_in)
    run(first, steps[0])
    total = sample_norms[:1, :] + centre_norms[...] - 2.0 * inner[...]
    r_all[0, :, :COUNT] = jnp.exp((2.0 * F - total) / (4.0 * math.sqrt(F))).astype(jnp.bfloat16)
    second = copies_of(plans[1], out_sems, in_sems)
    for kind, what in steps[1]:
        if kind != "start":
            break
        second[what].start()
    for copy in first:
        copy.wait_send()

    @pl.loop(0, o_ref.shape[0] // 3)
    def _(m):
        for n in range(3):
            k = m * 3 + n
            i, j = table[0, k], table[1, k]
            row_i, col_i, half_i = i >> 5, (i >> 1) & 15, i & 1
            row_j, col_j, half_j = j >> 5, (j >> 1) & 15, j & 1

            def far_col(c):
                return (((c >> 1) - z) & 7) * 2 + ((c + core) & 1)

            left = left_place((row_j - x) & 3, half_j, far_col(col_i), half_i)
            right = right_place(far_col(col_j), half_j, ((row_i - x) & 3) * 2 + half_i)
            straight = jnp.logical_and(row_i == x, col_j == col)
            place_of[k] = right + (left - right) * straight.astype(jnp.int32)

    begin = [k for k, (kind, _) in enumerate(steps[1]) if kind != "start"][0]
    run(second, steps[1][begin:])
    for copy in second:
        copy.wait_send()

    @pl.loop(0, o_ref.shape[0] // 3)
    def _(m):
        for n in range(3):
            k = m * 3 + n
            o_ref[k] = blocks[place_of[k]] * (1.0 / (N_SA * COUNT))


def normal_tiles(table, pick, states, pool):
    first, first_tasks = gather_inputs_plan()
    second, second_tasks = spread_plan()
    steps = [timetable(first, first_tasks, 1.5)[0], timetable(second, second_tasks, None)[0]]
    whole = N_SA * COUNT
    smem, anywhere = pl.BlockSpec(memory_space=pltpu.SMEM), pl.BlockSpec(memory_space=pl.ANY)
    return pl.pallas_call(
        functools.partial(normal_kernel, [first, second], steps),
        out_shape=jax.ShapeDtypeStruct((table.shape[1], QUART, MB), jnp.float32),
        in_specs=[smem, smem, anywhere, anywhere],
        out_specs=pl.BlockSpec(memory_space=pltpu.VMEM),
        scratch_shapes=[
            pltpu.VMEM((N_COL, CENT, whole), jnp.bfloat16),
            pltpu.VMEM((N_ROW - 1, CENT, whole), jnp.bfloat16),
            pltpu.VMEM((2 * 2 * N_ROW * 2 * N_COL, QUART, MB), jnp.float32),
            pltpu.VMEM((CENT, whole), jnp.bfloat16),
            pltpu.VMEM((CENT, COUNT), jnp.bfloat16),
            pltpu.VMEM((N_SA, COUNT, FEAT), jnp.float32),
            pltpu.VMEM((N_SA, CENT, FEAT), jnp.float32),
            pltpu.VMEM((2, SHARE // 2, FEAT), jnp.float32),
            pltpu.VMEM(pool.shape, jnp.float32),
            pltpu.VMEM((CENT, COUNT), jnp.float32),
            pltpu.VMEM((8, COUNT), jnp.float32),
            pltpu.VMEM((CENT, 1), jnp.float32),
            pltpu.SMEM((table.shape[1],), jnp.int32),
            pltpu.SemaphoreType.DMA((2,)),
            pltpu.SemaphoreType.DMA((len(first),)),
            pltpu.SemaphoreType.DMA((len(first),)),
            pltpu.SemaphoreType.DMA((len(second),)),
            pltpu.SemaphoreType.DMA((len(second),)),
        ],
        compiler_params=pltpu.CompilerParams(
            collective_id=0, has_side_effects=True, vmem_limit_bytes=56 * 2**20
        ),
    )(table, pick, states, pool)


def shards(states, pool, pick, tile_table):
    return normal_tiles(tile_table.T, pick, states, pool)


def solution(mesh):
    placed = (P(None, "sa"), P(("row", "col"), "sa"), P(("row", "col")), P(("row", "col"), None))
    return jax.shard_map(
        shards, mesh=mesh, in_specs=placed, out_specs=P(("row", "col"), "sa", None), check_vma=False
    )
```

```python
import functools
import heapq
import math

import jax
import jax.numpy as jnp
from jax import lax
from jax.experimental import pallas as pl
from jax.experimental.pallas import tpu as pltpu
from jax.sharding import PartitionSpec as P

F = 1024
M = 16384
MB = 128
N_SA = 4
N_ROW = 4
N_COL = 16
N_Z = 8
QUART = MB // N_SA
CENT = 256
COUNT = 640
POOL_DEV = 512
FEAT = F // N_SA
SPLIT = 384
Z_FIRST = (0, SPLIT)
Y_FIRST = (SPLIT, COUNT)
EVERY = (0, COUNT)
WINDOWS = (Z_FIRST, Y_FIRST)
PIECES = 3
GROUPS = ((0, 1, 2, 14), (3, 15, 4, 12), (5, 13, 6, 10), (7, 11, 8, 9))
RATE = {"s": 300e3}
LINK_RATE = 45e3
LATENCY = 1.7


class Send:
    def __init__(self, link, src, dst, size, deps, rank):
        self.link, self.src, self.dst, self.size = link, src, dst, size
        self.deps, self.rank = tuple(deps), rank


def ring(sends, axis, size, unit, own, halves, nbytes, deps, rank):
    filled = {}
    for sign, half in (("+", halves[0]), ("-", halves[1])):
        step = -1 if sign == "+" else 1
        need, at = deps, 0
        for hop in range(1, size // 2 + 1):
            last = hop == size // 2
            part = half if last else None
            to = (at + step) % size
            src = own(part) if at == 0 else unit(at, part)
            sends.append(Send(axis + sign, src, unit(to, part), nbytes // 2 if last else nbytes, need, rank + hop))
            filled.setdefault(to, []).append(len(sends) - 1)
            need, at = [len(sends) - 1], to
    return filled


def share_of(w):
    return (WINDOWS[w][1] - WINDOWS[w][0]) // 8


def inputs_plan(sends, tasks):
    row_bytes = 4 * FEAT

    def add(*args):
        sends.append(Send(*args))
        return len(sends) - 1

    relays = []
    for w in range(2):
        half = share_of(w) // 2
        need = ("local", *relays) if w else ()
        relays.append(add("y+", ("H", 2, w, 0, half), ("B", 2 * w, half), half * row_bytes, need, 4 * w))
        relays.append(add("y-", ("H", 2, w, half, half), ("B", 2 * w + 1, half), half * row_bytes, need, 4 * w))
    states, late = {}, ((), ("local", *relays[:2]))
    for w in range(2):
        share = share_of(w)
        half = share // 2
        come = {3: [add("y+", ("H", 1, w, 0, share), ("S", 3, 0, w, 0, share), share * row_bytes, late[w], 1 + 4 * w)],
                1: [add("y-", ("H", 3, w, 0, share), ("S", 1, 0, w, 0, share), share * row_bytes, late[w], 1 + 4 * w)]}
        come[2] = [add("y+", ("B", 2 * w, half), ("S", 2, 0, w, 0, half), half * row_bytes, [relays[2 * w]], 0),
                   add("y-", ("B", 2 * w + 1, half), ("S", 2, 0, w, half, half), half * row_bytes, [relays[2 * w + 1]], 0)]

        def rows(part):
            return (0, share) if part is None else part

        for d in (3, 1, 2):
            got = ring(sends, "x", N_ROW, lambda dx, part: ("S", d, dx, w, *rows(part)),
                       lambda part: ("S", d, 0, w, *rows(part)), ((0, half), (half, half)), share * row_bytes, come[d], 0)
            got[0] = come[d]
            states[d, w] = [k for dx in range(N_ROW) for k in got[dx]]
            for dx in (0, 3, 1, 2):
                place = ("S", d, dx, w, 0, share)
                states[d, w].append(add("s", place, place, share * row_bytes, got[dx], 5))

    def cent(part):
        return (0, CENT) if part is None else part

    halves = ((0, CENT // 2), (CENT // 2, CENT // 2))
    centres = ring(sends, "y", N_SA, lambda d, part: ("F", d, *cent(part)), lambda part: ("F", 0, *cent(part)), halves,
                   CENT * row_bytes, ("local", *relays[:2]), 3)
    tasks.append(("local", None, (), 1.5, True))
    for w in range(2):
        tasks.append(("distance", (0, w), ("local",), 0.5, False))
    for n in range(PIECES):
        tasks.append(("places", n, ("local",), 0.8, False))
    for w in range(2):
        for d in (3, 1, 2):
            tasks.append(("distance", (d, w), tuple(states[d, w] + centres[d]), 0.5, True))
        tasks.append(("kernel", w, tuple(("distance", (d, w)) for d in range(N_SA)), 0.3, True))


def spread_plan(sends, tasks):
    kernels = [("kernel", w) for w in range(2)]

    def cut(cols, half):
        first, rows = (0, CENT) if half is None else half
        return (first, rows, cols[0], cols[1] - cols[0])

    halves = ((0, CENT // 2), (CENT // 2, CENT // 2))

    def area(cols):
        return 2 * CENT * (cols[1] - cols[0])

    def r_ring(axis, size, place, cols, deps, rank):
        return ring(sends, axis, size, lambda d, half: ("R", *place(d), 0, cut(cols, half)),
                    lambda half: ("R", *place(0), 0, cut(cols, half)), halves, area(cols), deps, rank)

    z_own = r_ring("z", N_Z, lambda d: (0, d), Z_FIRST, kernels[:1], 6)
    y_own = [r_ring("y", N_SA, lambda d: (d, 0), WINDOWS[w], kernels[w:w + 1], 6) for w in range(2)]
    arrived = {}
    for dz in range(1, N_Z):
        arrived[0, dz, Z_FIRST] = z_own[dz]
        got = r_ring("y", N_SA, lambda d: (d, dz), Z_FIRST, z_own[dz], 10)
        for dy in range(1, N_SA):
            arrived[dy, dz, Z_FIRST] = got[dy]
    in_r, in_c = {(dy, 0): y_own[0][dy] + y_own[1][dy] if dy else kernels for dy in range(N_SA)}, {}
    for dy in range(N_SA):
        need = in_r[dy, 0]
        got = r_ring("z", N_Z, lambda d: (dy, d), Y_FIRST, y_own[1][dy] if dy else kernels[1:], 10)
        for dz in range(1, N_Z):
            arrived[dy, dz, Y_FIRST] = got[dz]
        got = ring(sends, "x", N_ROW, lambda d, half: ("C", dy, d, cut(EVERY, half)),
                   lambda half: ("R", dy, 0, 0, cut(EVERY, half)), halves, area(EVERY), need, 20)
        in_c[dy] = [k for ks in got.values() for k in ks] + need
        sends.append(Send("s", ("R", dy, 0, 0, cut(EVERY, None)), ("R", dy, 0, 1, cut(EVERY, None)), area(EVERY), need, 30))
        in_r[dy, 1] = [len(sends) - 1]
    for (dy, dz, cols), need in arrived.items():
        sends.append(Send("s", ("R", dy, dz, 0, cut(cols, None)), ("R", dy, dz, 1, cut(cols, None)), area(cols), need, 30))
        in_r.setdefault((dy, dz * 2), []).extend(need)
        in_r.setdefault((dy, dz * 2 + 1), []).append(len(sends) - 1)

    for dy in range(N_SA):
        tasks.append(("columns", dy, tuple(in_c[dy]), 0.15, False))
    for group in GROUPS:
        for dy in range(N_SA):
            need = [k for slot in group for k in in_r[dy, slot]] + in_c[dy]
            tasks.append(("right", (group, dy), (*need, ("columns", dy)), 0.5, False))
            tasks.append(("left", (group, dy), tuple(need), 0.5, False))


def timetable(sends, tasks):
    free, pending, done, queue, steps = {}, set(range(len(sends))), set(), [], []
    undone = list(range(len(tasks)))

    def start_ready(now):
        ready = sorted((k for k in pending if all(d in done for d in sends[k].deps)), key=lambda k: (sends[k].rank, k))
        for k in ready:
            pending.discard(k)
            link = sends[k].link
            free[link] = max(now, free.get(link, 0.0)) + sends[k].size / RATE.get(link, LINK_RATE)
            heapq.heappush(queue, (free[link] + LATENCY, k))
            steps.append(("start", k))

    core = 0.0
    start_ready(core)
    while queue or undone:
        coming = queue[0][0] if queue else math.inf
        ready = [t for t in undone if all(d in done for d in tasks[t][2])]
        ready.sort(key=lambda t: not tasks[t][4])
        if ready and coming - core >= (0.0 if tasks[ready[0]][4] else 0.6 * tasks[ready[0]][3]):
            kind, what, _, span, _ = tasks[ready[0]]
            undone.remove(ready[0])
            core += span
            steps.append((kind, what))
            done.add(kind if what is None else (kind, what))
            start_ready(core)
            continue
        now, k = heapq.heappop(queue)
        core = max(core, now)
        done.add(k)
        steps.append(("wait", k))
        start_ready(core)
    return steps, core


def left_place(dev, half, slot, slot_half):
    return (dev * 2 + half) * 2 * N_COL + slot * 2 + slot_half


def right_place(slot, half, place):
    return 2 * N_ROW * 2 * N_COL + (slot * 2 + half) * 2 * N_ROW + place


def normal_kernel(sends, steps, table, pick, states, pool, out, r_all, c_all, blocks, cq, rq, s_all, f_all, relay,
                  pool_local, inner, centre_norms, place_of, o_ref, copy_sems, out_sems, in_sems):
    y, x, col = lax.axis_index("sa"), lax.axis_index("row"), lax.axis_index("col")
    z, core = col // 2, col % 2
    to = {
        "y+": {"sa": (y + 1) % N_SA},
        "y-": {"sa": (y + 3) % N_SA},
        "x+": {"row": (x + 1) % N_ROW},
        "x-": {"row": (x + 3) % N_ROW},
        "z+": {"col": (z + 1) % N_Z * 2 + core},
        "z-": {"col": (z + 7) % N_Z * 2 + core},
        "s": {"col": z * 2 + 1 - core},
    }
    mesh_id = pl.DeviceIdType.MESH
    pool_copy = pltpu.make_async_copy(pool, pool_local, copy_sems.at[0])
    pool_copy.start()
    states_copy = pltpu.make_async_copy(
        states.at[pl.ds(pl.multiple_of(y * COUNT, COUNT), COUNT), :], s_all.at[0], copy_sems.at[1])
    states_copy.start()
    barrier = pltpu.get_barrier_semaphore()
    for peer in to.values():
        pl.semaphore_signal(barrier, inc=1, device_id=peer, device_id_type=mesh_id)
    pl.semaphore_wait(barrier, len(to))

    def place_ref(place):
        kind = place[0]
        if kind == "H":
            w = place[2]
            first = (y + place[1]) % N_SA * COUNT + WINDOWS[w][0] + (x * 2 + core) * share_of(w) + place[3]
            return states.at[pl.ds(pl.multiple_of(first, 8), place[4]), :]
        if kind == "B":
            return relay.at[place[1], pl.ds(0, place[2]), :]
        if kind == "S":
            w = place[3]
            first = WINDOWS[w][0] + ((x + place[2]) % N_ROW * 2 + core) * share_of(w) + place[4]
            return s_all.at[place[1], pl.ds(pl.multiple_of(first, 8), place[5]), :]
        if kind == "F":
            return f_all.at[place[1], pl.ds(place[2], place[3]), :]
        first, rows, start, count = place[-1]
        rows, cols = pl.ds(first, rows), pl.ds(place[1] * COUNT + start, count)
        if kind == "R":
            return r_all.at[place[2] * 2 + place[3], rows, cols]
        return c_all.at[place[2] - 1, rows, cols]

    def landing(send):
        if send.src[0] == "S":
            return place_ref(send.src)
        return place_ref(send.dst)

    copies = [
        pltpu.make_async_remote_copy(
            src_ref=place_ref(send.src), dst_ref=landing(send), send_sem=out_sems.at[k], recv_sem=in_sems.at[k],
            device_id=to[send.link], device_id_type=mesh_id)
        for k, send in enumerate(sends)
    ]

    def dot(left, right, precision=None):
        return lax.dot_general(left, right, (((1,), (1,)), ((), ())), precision=precision,
                               preferred_element_type=jnp.float32)

    begun = set()

    def put(ref, where, value, key):
        if key in begun:
            ref[where] += value
        else:
            ref[where] = value

    def distance(d, w):
        cols = slice(*WINDOWS[w])
        sample, centre = s_all[d, cols, :], f_all[d]
        squares = sample * sample
        squares = squares[:, :MB] + squares[:, MB:]
        norms = jnp.sum(squares.T, axis=0, keepdims=True)
        cross = dot(centre, sample, lax.Precision.HIGHEST)
        put(inner, (slice(None), cols), norms - 2.0 * cross, w)
        begun.add(w)
        if ("centre", d) not in begun:
            own = jnp.sum(centre * centre, axis=1, keepdims=True)
            put(centre_norms, (slice(None), slice(None)), own, "centres")
            begun.update(("centres", ("centre", d)))

    def kernel_values(w):
        cols = slice(*WINDOWS[w])
        total = inner[:, cols] + centre_norms[...]
        r_all[0, :, cols] = jnp.exp((2.0 * F - total) / (4.0 * math.sqrt(F))).astype(jnp.bfloat16)

    def places(piece):
        size = out.shape[0] // PIECES

        @pl.loop(0, size)
        def _(m):
            k = piece * size + m
            i, j = table[0, k], table[1, k]
            row_i, col_i, half_i = i >> 5, (i >> 1) & 15, i & 1
            row_j, col_j, half_j = j >> 5, (j >> 1) & 15, j & 1

            def far_col(c):
                return (((c >> 1) - z) & 7) * 2 + ((c + core) & 1)

            left = left_place((row_j - x) & 3, half_j, far_col(col_i), half_i)
            right = right_place(far_col(col_j), half_j, ((row_i - x) & 3) * 2 + half_i)
            straight = jnp.logical_and(row_i == x, col_j == col)
            place_of[k] = right + (left - right) * straight.astype(jnp.int32)

    def local():
        pool_copy.wait()

        @pl.loop(0, CENT // 8)
        def _(m):
            for n in range(8):
                f_all[0, m * 8 + n] = pool_local[pick[m * 8 + n] & (POOL_DEV - 1)]

        states_copy.wait()

    def column(dev):
        return c_all.at[dev - 1] if dev else r_all.at[0]

    def quarter(half):
        return pl.ds(pl.multiple_of(half * MB + y * QUART, QUART), QUART)

    def task(kind, what):
        if kind == "columns":
            cols = slice(what * COUNT, (what + 1) * COUNT)
            for dev in range(N_ROW):
                for half in range(2):
                    top = (dev * 2 + half) * QUART
                    cq[top:top + QUART, cols] = column(dev)[quarter(half), cols]
            return
        group, dy = what
        cols = slice(dy * COUNT, (dy + 1) * COUNT)
        if kind == "right":
            for slot in group:
                got = dot(cq[:, cols], r_all[slot, :, cols])
                for half in range(2):
                    for n in range(2 * N_ROW):
                        put(blocks, right_place(slot, half, n), got[n * QUART:(n + 1) * QUART, half * MB:(half + 1) * MB],
                            (kind, group))
        else:
            for n, slot in enumerate(group):
                for half in range(2):
                    top = (n * 2 + half) * QUART
                    rq[top:top + QUART, :] = r_all[slot, quarter(half), cols]
            for dev in range(N_ROW):
                got = dot(rq[...], column(dev)[:, cols])
                for half in range(2):
                    for n in range(8):
                        put(blocks, left_place(dev, half, group[n // 2], n % 2),
                            got[n * QUART:(n + 1) * QUART, half * MB:(half + 1) * MB], (kind, group))
        begun.add((kind, group))

    for kind, what in steps:
        if kind == "wait":
            copies[what].wait_recv()
        elif kind == "start":
            copies[what].start()
        elif kind == "local":
            local()
        elif kind == "distance":
            distance(*what)
        elif kind == "kernel":
            kernel_values(what)
        elif kind == "places":
            places(what)
        else:
            task(kind, what)

    size = out.shape[0] // PIECES
    results = []
    for piece in range(PIECES):
        @pl.loop(0, size)
        def _(m):
            k = piece * size + m
            o_ref[k] = blocks[place_of[k]] * (1.0 / (N_SA * COUNT))

        part = pl.ds(piece * size, size)
        results.append(pltpu.make_async_copy(o_ref.at[part], out.at[part], copy_sems.at[2 + piece]))
        results[-1].start()
    for copy in copies:
        copy.wait_send()
    for copy in results:
        copy.wait()


def normal_tiles(table, pick, states, pool):
    sends, tasks = [], []
    inputs_plan(sends, tasks)
    spread_plan(sends, tasks)
    steps, _ = timetable(sends, tasks)
    whole = N_SA * COUNT
    smem, hbm, anywhere = (pl.BlockSpec(memory_space=space) for space in (pltpu.SMEM, pltpu.HBM, pl.ANY))
    return pl.pallas_call(
        functools.partial(normal_kernel, sends, steps),
        out_shape=jax.ShapeDtypeStruct((table.shape[1], QUART, MB), jnp.float32),
        in_specs=[smem, smem, hbm, hbm],
        out_specs=anywhere,
        scratch_shapes=[
            pltpu.VMEM((N_COL, CENT, whole), jnp.bfloat16),
            pltpu.VMEM((N_ROW - 1, CENT, whole), jnp.bfloat16),
            pltpu.VMEM((2 * 2 * N_ROW * 2 * N_COL, QUART, MB), jnp.float32),
            pltpu.VMEM((CENT, whole), jnp.bfloat16),
            pltpu.VMEM((CENT, COUNT), jnp.bfloat16),
            pltpu.VMEM((N_SA, COUNT, FEAT), jnp.float32),
            pltpu.VMEM((N_SA, CENT, FEAT), jnp.float32),
            pltpu.VMEM((4, share_of(0) // 2, FEAT), jnp.float32),
            pltpu.VMEM(pool.shape, jnp.float32),
            pltpu.VMEM((CENT, COUNT), jnp.float32),
            pltpu.VMEM((CENT, 1), jnp.float32),
            pltpu.SMEM((table.shape[1],), jnp.int32),
            pltpu.VMEM((table.shape[1], QUART, MB), jnp.float32),
            pltpu.SemaphoreType.DMA((2 + PIECES,)),
            pltpu.SemaphoreType.DMA((len(sends),)),
            pltpu.SemaphoreType.DMA((len(sends),)),
        ],
        compiler_params=pltpu.CompilerParams(
            collective_id=0, has_side_effects=True, vmem_limit_bytes=46 * 2**20
        ),
    )(table, pick, states, pool)


def shards(states, pool, pick, tile_table):
    return normal_tiles(tile_table.T, pick, states, pool)


def solution(mesh):
    placed = (P(None, "sa"), P(("row", "col"), "sa"), P(("row", "col")), P(("row", "col"), None))
    return jax.shard_map(
        shards, mesh=mesh, in_specs=placed, out_specs=P(("row", "col"), "sa", None), check_vma=False
    )
```

```python
import functools
import heapq
import math

import jax
import jax.numpy as jnp
from jax import lax
from jax.experimental import pallas as pl
from jax.experimental.pallas import tpu as pltpu
from jax.sharding import PartitionSpec as P

F = 1024
M = 16384
MB = 128
N_SA = 4
N_ROW = 4
N_COL = 16
N_Z = 8
QUART = MB // N_SA
CENT = 256
COUNT = 640
POOL_DEV = 512
FEAT = F // N_SA
SPLIT = 384
Z_FIRST = (0, SPLIT)
Y_FIRST = (SPLIT, COUNT)
EVERY = (0, COUNT)
WINDOWS = (Z_FIRST, Y_FIRST)
PIECES = 3
GROUPS = ((0, 1, 2, 14), (3, 15, 4, 12), (5, 13, 6, 10), (7, 11, 8, 9))
RATE = {"s": 300e3}
LINK_RATE = 45e3
LATENCY = 1.7
LEAF = 3.0


class Send:
    def __init__(self, link, src, dst, size, deps, rank):
        self.link, self.src, self.dst, self.size = link, src, dst, size
        self.deps, self.rank = tuple(deps), rank


def ring(sends, axis, size, unit, own, halves, nbytes, deps, rank):
    filled = {}
    for sign, half in (("+", halves[0]), ("-", halves[1])):
        step = -1 if sign == "+" else 1
        need, at = deps, 0
        for hop in range(1, size // 2 + 1):
            last = hop == size // 2
            part = half if last else None
            to = (at + step) % size
            src = own(part) if at == 0 else unit(at, part)
            sends.append(Send(axis + sign, src, unit(to, part), nbytes // 2 if last else nbytes, need, rank + hop))
            filled.setdefault(to, []).append(len(sends) - 1)
            need, at = [len(sends) - 1], to
    return filled


def share_of(w):
    return (WINDOWS[w][1] - WINDOWS[w][0]) // 8


def inputs_plan(sends, tasks):
    row_bytes = 4 * FEAT

    def add(*args):
        sends.append(Send(*args))
        return len(sends) - 1

    relays = []
    for w in range(2):
        half = share_of(w) // 2
        relays.append(add("y+", ("H", 2, w, 0, half), ("B", 2 * w, half), half * row_bytes, (), 0))
        relays.append(add("y-", ("H", 2, w, half, half), ("B", 2 * w + 1, half), half * row_bytes, (), 0))
    states = {}
    for w in range(2):
        share = share_of(w)
        half = share // 2
        come = {3: [add("y+", ("H", 1, w, 0, share), ("S", 3, 0, w, 0, share), share * row_bytes, (), 1 + w)],
                1: [add("y-", ("H", 3, w, 0, share), ("S", 1, 0, w, 0, share), share * row_bytes, (), 1 + w)]}
        come[2] = [add("y+", ("B", 2 * w, half), ("S", 2, 0, w, 0, half), half * row_bytes, [relays[2 * w]], 0),
                   add("y-", ("B", 2 * w + 1, half), ("S", 2, 0, w, half, half), half * row_bytes, [relays[2 * w + 1]], 0)]

        def rows(part):
            return (0, share) if part is None else part

        for d in (3, 1, 2):
            got = ring(sends, "x", N_ROW, lambda dx, part: ("S", d, dx, w, *rows(part)),
                       lambda part: ("S", d, 0, w, *rows(part)), ((0, half), (half, half)), share * row_bytes, come[d], 0)
            got[0] = come[d]
            states[d, w] = [k for dx in range(N_ROW) for k in got[dx]]
            for dx in (0, 3, 1, 2):
                place = ("S", d, dx, w, 0, share)
                states[d, w].append(add("s", place, place, share * row_bytes, got[dx], 5))

    def cent(part):
        return (0, CENT) if part is None else part

    halves = ((0, CENT // 2), (CENT // 2, CENT // 2))
    centres = ring(sends, "y", N_SA, lambda d, part: ("F", d, *cent(part)), lambda part: ("F", 0, *cent(part)), halves,
                   CENT * row_bytes, ("local", *relays), 3)
    tasks.append(("local", None, (), 1.5, True))
    for w in range(2):
        tasks.append(("distance", (0, w), ("local",), 0.5, False))
    for n in range(PIECES):
        tasks.append(("places", n, ("local",), 0.8, False))
    for w in range(2):
        for d in (3, 1, 2):
            need = (*states[d, w], *centres[d], *([("kernel", 0)] if w else []))
            tasks.append(("distance", (d, w), need, 0.5, True))
        tasks.append(("kernel", w, tuple(("distance", (d, w)) for d in range(N_SA)), 0.3, True))


def spread_plan(sends, tasks):
    kernels = [("kernel", w) for w in range(2)]

    def cut(cols, half):
        first, rows = (0, CENT) if half is None else half
        return (first, rows, cols[0], cols[1] - cols[0])

    halves = ((0, CENT // 2), (CENT // 2, CENT // 2))

    def area(cols):
        return 2 * CENT * (cols[1] - cols[0])

    def r_ring(axis, size, place, cols, deps, rank):
        return ring(sends, axis, size, lambda d, half: ("R", *place(d), 0, cut(cols, half)),
                    lambda half: ("R", *place(0), 0, cut(cols, half)), halves, area(cols), deps, rank)

    z_own = r_ring("z", N_Z, lambda d: (0, d), Z_FIRST, kernels[:1], 6)
    y_own = [r_ring("y", N_SA, lambda d: (d, 0), WINDOWS[w], kernels[w:w + 1], 6) for w in range(2)]
    arrived = {}
    for dz in range(1, N_Z):
        arrived[0, dz, Z_FIRST] = z_own[dz]
        got = r_ring("y", N_SA, lambda d: (d, dz), Z_FIRST, z_own[dz], 10)
        for dy in range(1, N_SA):
            arrived[dy, dz, Z_FIRST] = got[dy]
    in_r, in_c = {(dy, 0): y_own[0][dy] + y_own[1][dy] if dy else kernels for dy in range(N_SA)}, {}
    for dy in range(N_SA):
        need = in_r[dy, 0]
        got = r_ring("z", N_Z, lambda d: (dy, d), Y_FIRST, y_own[1][dy] if dy else kernels[1:], 10)
        for dz in range(1, N_Z):
            arrived[dy, dz, Y_FIRST] = got[dz]
        got = ring(sends, "x", N_ROW, lambda d, half: ("C", dy, d, cut(EVERY, half)),
                   lambda half: ("R", dy, 0, 0, cut(EVERY, half)), halves, area(EVERY), need, 20)
        in_c[dy] = [k for ks in got.values() for k in ks] + need
        sends.append(Send("s", ("R", dy, 0, 0, cut(EVERY, None)), ("R", dy, 0, 1, cut(EVERY, None)), area(EVERY), need, 30))
        in_r[dy, 1] = [len(sends) - 1]
    for (dy, dz, cols), need in arrived.items():
        halved = dz == N_Z // 2 if dy == 0 or cols == Y_FIRST else dy == N_SA // 2
        for k in need if halved else [None]:
            part = cut(cols, None) if k is None else sends[k].dst[-1]
            size = area(cols) if k is None else sends[k].size
            sends.append(Send("s", ("R", dy, dz, 0, part), ("R", dy, dz, 1, part), size, need if k is None else [k], 30))
            in_r.setdefault((dy, dz * 2 + 1), []).append(len(sends) - 1)
        in_r.setdefault((dy, dz * 2), []).extend(need)

    for dy in range(N_SA):
        tasks.append(("columns", dy, tuple(in_c[dy]), 0.15, False))
    for group in GROUPS:
        for dy in range(N_SA):
            need = [k for slot in group for k in in_r[dy, slot]] + in_c[dy]
            tasks.append(("right", (group, dy), (*need, ("columns", dy)), 0.5, False))
            tasks.append(("left", (group, dy), tuple(need), 0.5, False))


def timetable(sends, tasks):
    free, pending, done, queue, steps = {}, set(range(len(sends))), set(), [], []
    undone = list(range(len(tasks)))
    relayed = {d for send in sends for d in send.deps} | {d for t in tasks if t[4] for d in t[2]}

    def start_ready(now):
        ready = sorted((k for k in pending if all(d in done for d in sends[k].deps)), key=lambda k: (sends[k].rank, k))
        for k in ready:
            pending.discard(k)
            link = sends[k].link
            free[link] = max(now, free.get(link, 0.0)) + sends[k].size / RATE.get(link, LINK_RATE)
            heapq.heappush(queue, (free[link] + LATENCY + (0.0 if k in relayed else LEAF), k))
            steps.append(("start", k))

    core = 0.0
    start_ready(core)
    while queue or undone:
        coming = queue[0][0] if queue else math.inf
        ready = [t for t in undone if all(d in done for d in tasks[t][2])]
        ready.sort(key=lambda t: not tasks[t][4])
        if ready and coming - core >= (0.0 if tasks[ready[0]][4] else 0.6 * tasks[ready[0]][3]):
            kind, what, _, span, _ = tasks[ready[0]]
            undone.remove(ready[0])
            core += span
            steps.append((kind, what))
            done.add(kind if what is None else (kind, what))
            start_ready(core)
            continue
        now, k = heapq.heappop(queue)
        core = max(core, now)
        done.add(k)
        steps.append(("wait", k))
        start_ready(core)
    return steps, core


def left_place(dev, half, slot, slot_half):
    return (dev * 2 + half) * 2 * N_COL + slot * 2 + slot_half


def right_place(slot, half, place):
    return 2 * N_ROW * 2 * N_COL + (slot * 2 + half) * 2 * N_ROW + place


def normal_kernel(sends, steps, table, pick, states, pool, out, r_all, c_all, blocks, cq, rq, s_all, f_all, relay,
                  pool_local, inner, centre_norms, place_of, o_ref, copy_sems, out_sems, in_sems):
    y, x, col = lax.axis_index("sa"), lax.axis_index("row"), lax.axis_index("col")
    z, core = col // 2, col % 2
    to = {
        "y+": {"sa": (y + 1) % N_SA},
        "y-": {"sa": (y + 3) % N_SA},
        "x+": {"row": (x + 1) % N_ROW},
        "x-": {"row": (x + 3) % N_ROW},
        "z+": {"col": (z + 1) % N_Z * 2 + core},
        "z-": {"col": (z + 7) % N_Z * 2 + core},
        "s": {"col": z * 2 + 1 - core},
    }
    mesh_id = pl.DeviceIdType.MESH
    pool_copy = pltpu.make_async_copy(pool, pool_local, copy_sems.at[0])
    pool_copy.start()
    states_copy = pltpu.make_async_copy(
        states.at[pl.ds(pl.multiple_of(y * COUNT, COUNT), COUNT), :], s_all.at[0], copy_sems.at[1])
    states_copy.start()
    barrier = pltpu.get_barrier_semaphore()
    for peer in to.values():
        pl.semaphore_signal(barrier, inc=1, device_id=peer, device_id_type=mesh_id)
    pl.semaphore_wait(barrier, len(to))

    def place_ref(place):
        kind = place[0]
        if kind == "H":
            w = place[2]
            first = (y + place[1]) % N_SA * COUNT + WINDOWS[w][0] + (x * 2 + core) * share_of(w) + place[3]
            return states.at[pl.ds(pl.multiple_of(first, 8), place[4]), :]
        if kind == "B":
            return relay.at[place[1], pl.ds(0, place[2]), :]
        if kind == "S":
            w = place[3]
            first = WINDOWS[w][0] + ((x + place[2]) % N_ROW * 2 + core) * share_of(w) + place[4]
            return s_all.at[place[1], pl.ds(pl.multiple_of(first, 8), place[5]), :]
        if kind == "F":
            return f_all.at[place[1], pl.ds(place[2], place[3]), :]
        first, rows, start, count = place[-1]
        rows, cols = pl.ds(first, rows), pl.ds(place[1] * COUNT + start, count)
        if kind == "R":
            return r_all.at[place[2] * 2 + place[3], rows, cols]
        return c_all.at[place[2] - 1, rows, cols]

    def landing(send):
        if send.src[0] == "S":
            return place_ref(send.src)
        return place_ref(send.dst)

    copies = [
        pltpu.make_async_remote_copy(
            src_ref=place_ref(send.src), dst_ref=landing(send), send_sem=out_sems.at[k], recv_sem=in_sems.at[k],
            device_id=to[send.link], device_id_type=mesh_id)
        for k, send in enumerate(sends)
    ]

    def dot(left, right, precision=None):
        return lax.dot_general(left, right, (((1,), (1,)), ((), ())), precision=precision,
                               preferred_element_type=jnp.float32)

    begun = set()

    def put(ref, where, value, key):
        if key in begun:
            ref[where] += value
        else:
            ref[where] = value

    def distance(d, w):
        cols = slice(*WINDOWS[w])
        sample, centre = s_all[d, cols, :], f_all[d]
        squares = sample * sample
        squares = squares[:, :MB] + squares[:, MB:]
        norms = jnp.sum(squares.T, axis=0, keepdims=True)
        cross = dot(centre, sample, lax.Precision.HIGHEST)
        put(inner, (slice(None), cols), norms - 2.0 * cross, w)
        begun.add(w)
        if ("centre", d) not in begun:
            own = jnp.sum(centre * centre, axis=1, keepdims=True)
            put(centre_norms, (slice(None), slice(None)), own, "centres")
            begun.update(("centres", ("centre", d)))

    def kernel_values(w):
        cols = slice(*WINDOWS[w])
        total = inner[:, cols] + centre_norms[...]
        r_all[0, :, cols] = jnp.exp((2.0 * F - total) / (4.0 * math.sqrt(F))).astype(jnp.bfloat16)

    def places(piece):
        size = out.shape[0] // PIECES

        @pl.loop(0, size)
        def _(m):
            k = piece * size + m
            i, j = table[0, k], table[1, k]
            row_i, col_i, half_i = i >> 5, (i >> 1) & 15, i & 1
            row_j, col_j, half_j = j >> 5, (j >> 1) & 15, j & 1

            def far_col(c):
                return (((c >> 1) - z) & 7) * 2 + ((c + core) & 1)

            left = left_place((row_j - x) & 3, half_j, far_col(col_i), half_i)
            right = right_place(far_col(col_j), half_j, ((row_i - x) & 3) * 2 + half_i)
            straight = jnp.logical_and(row_i == x, col_j == col)
            place_of[k] = right + (left - right) * straight.astype(jnp.int32)

    def local():
        pool_copy.wait()

        @pl.loop(0, CENT // 8)
        def _(m):
            for n in range(8):
                f_all[0, m * 8 + n] = pool_local[pick[m * 8 + n] & (POOL_DEV - 1)]

        states_copy.wait()

    def column(dev):
        return c_all.at[dev - 1] if dev else r_all.at[0]

    def quarter(half):
        return pl.ds(pl.multiple_of(half * MB + y * QUART, QUART), QUART)

    def task(kind, what):
        if kind == "columns":
            cols = slice(what * COUNT, (what + 1) * COUNT)
            for dev in range(N_ROW):
                for half in range(2):
                    top = (dev * 2 + half) * QUART
                    cq[top:top + QUART, cols] = column(dev)[quarter(half), cols]
            return
        group, dy = what
        cols = slice(dy * COUNT, (dy + 1) * COUNT)
        if kind == "right":
            for slot in group:
                got = dot(cq[:, cols], r_all[slot, :, cols])
                for half in range(2):
                    for n in range(2 * N_ROW):
                        put(blocks, right_place(slot, half, n), got[n * QUART:(n + 1) * QUART, half * MB:(half + 1) * MB],
                            (kind, group))
        else:
            for n, slot in enumerate(group):
                for half in range(2):
                    top = (n * 2 + half) * QUART
                    rq[top:top + QUART, :] = r_all[slot, quarter(half), cols]
            for dev in range(N_ROW):
                got = dot(rq[...], column(dev)[:, cols])
                for half in range(2):
                    for n in range(8):
                        put(blocks, left_place(dev, half, group[n // 2], n % 2),
                            got[n * QUART:(n + 1) * QUART, half * MB:(half + 1) * MB], (kind, group))
        begun.add((kind, group))

    for kind, what in steps:
        if kind == "wait":
            copies[what].wait_recv()
        elif kind == "start":
            copies[what].start()
        elif kind == "local":
            local()
        elif kind == "distance":
            distance(*what)
        elif kind == "kernel":
            kernel_values(what)
        elif kind == "places":
            places(what)
        else:
            task(kind, what)

    size = out.shape[0] // PIECES
    results = []
    for piece in range(PIECES):
        @pl.loop(0, size)
        def _(m):
            k = piece * size + m
            o_ref[k] = blocks[place_of[k]] * (1.0 / (N_SA * COUNT))

        part = pl.ds(piece * size, size)
        results.append(pltpu.make_async_copy(o_ref.at[part], out.at[part], copy_sems.at[2 + piece]))
        results[-1].start()
    for copy in copies:
        copy.wait_send()
    for copy in results:
        copy.wait()


def normal_tiles(table, pick, states, pool):
    sends, tasks = [], []
    inputs_plan(sends, tasks)
    spread_plan(sends, tasks)
    steps, _ = timetable(sends, tasks)
    whole = N_SA * COUNT
    smem, anywhere = pl.BlockSpec(memory_space=pltpu.SMEM), pl.BlockSpec(memory_space=pl.ANY)
    return pl.pallas_call(
        functools.partial(normal_kernel, sends, steps),
        out_shape=jax.ShapeDtypeStruct((table.shape[1], QUART, MB), jnp.float32),
        in_specs=[smem, smem, anywhere, anywhere],
        out_specs=anywhere,
        scratch_shapes=[
            pltpu.VMEM((N_COL, CENT, whole), jnp.bfloat16),
            pltpu.VMEM((N_ROW - 1, CENT, whole), jnp.bfloat16),
            pltpu.VMEM((2 * 2 * N_ROW * 2 * N_COL, QUART, MB), jnp.float32),
            pltpu.VMEM((CENT, whole), jnp.bfloat16),
            pltpu.VMEM((CENT, COUNT), jnp.bfloat16),
            pltpu.VMEM((N_SA, COUNT, FEAT), jnp.float32),
            pltpu.VMEM((N_SA, CENT, FEAT), jnp.float32),
            pltpu.VMEM((4, share_of(0) // 2, FEAT), jnp.float32),
            pltpu.VMEM(pool.shape, jnp.float32),
            pltpu.VMEM((CENT, COUNT), jnp.float32),
            pltpu.VMEM((CENT, 1), jnp.float32),
            pltpu.SMEM((table.shape[1],), jnp.int32),
            pltpu.VMEM((table.shape[1], QUART, MB), jnp.float32),
            pltpu.SemaphoreType.DMA((2 + PIECES,)),
            pltpu.SemaphoreType.DMA((len(sends),)),
            pltpu.SemaphoreType.DMA((len(sends),)),
        ],
        compiler_params=pltpu.CompilerParams(
            collective_id=0, has_side_effects=True, vmem_limit_bytes=56 * 2**20
        ),
    )(table, pick, states, pool)


def shards(states, pool, pick, tile_table):
    return normal_tiles(tile_table.T, pick, states, pool)


def solution(mesh):
    placed = (P(None, "sa"), P(("row", "col"), "sa"), P(("row", "col")), P(("row", "col"), None))
    return jax.shard_map(
        shards, mesh=mesh, in_specs=placed, out_specs=P(("row", "col"), "sa", None), check_vma=False
    )
```

```python
import functools
import heapq
import math

import jax
import jax.numpy as jnp
from jax import lax
from jax.experimental import pallas as pl
from jax.experimental.pallas import tpu as pltpu
from jax.sharding import PartitionSpec as P

F = 1024
M = 16384
MB = 128
N_SA = 4
N_ROW = 4
N_COL = 16
N_Z = 8
QUART = MB // N_SA
CENT = 256
COUNT = 640
POOL_DEV = 512
FEAT = F // N_SA
SHARE = COUNT // 8
SPLIT = 384
Z_FIRST = (0, SPLIT)
Y_FIRST = (SPLIT, COUNT)
EVERY = (0, COUNT)
GROUPS = ((0, 1, 2, 14), (3, 15, 4, 12), (5, 13, 6, 10), (7, 11, 8, 9))
RATE = {"s": 300e3}
LINK_RATE = 45e3
LATENCY = 1.7
LEAF = 3.0


class Send:
    def __init__(self, link, src, dst, size, deps, rank):
        self.link, self.src, self.dst, self.size = link, src, dst, size
        self.deps, self.rank = tuple(deps), rank


def ring(sends, axis, size, unit, own, halves, nbytes, deps, rank):
    filled = {}
    for sign, half in (("+", halves[0]), ("-", halves[1])):
        step = -1 if sign == "+" else 1
        need, at = deps, 0
        for hop in range(1, size // 2 + 1):
            last = hop == size // 2
            part = half if last else None
            to = (at + step) % size
            src = own(part) if at == 0 else unit(at, part)
            sends.append(Send(axis + sign, src, unit(to, part), nbytes // 2 if last else nbytes, need, rank + hop))
            filled.setdefault(to, []).append(len(sends) - 1)
            need, at = [len(sends) - 1], to
    return filled


def gather_inputs_plan():
    sends, tasks = [], []
    row_bytes = 4 * FEAT
    half = SHARE // 2

    def add(*args):
        sends.append(Send(*args))
        return len(sends) - 1

    relay = [add("y+", ("H", 2, 0, half), ("B", 0), half * row_bytes, (), 0),
             add("y-", ("H", 2, half, half), ("B", 1), half * row_bytes, (), 0)]
    come = {3: [add("y+", ("H", 1, 0, SHARE), ("S", 3, 0, 0, 0, SHARE), SHARE * row_bytes, (), 1)],
            1: [add("y-", ("H", 3, 0, SHARE), ("S", 1, 0, 0, 0, SHARE), SHARE * row_bytes, (), 1)]}
    come[2] = [add("y+", ("B", 0), ("S", 2, 0, 0, 0, half), half * row_bytes, relay[:1], 0),
               add("y-", ("B", 1), ("S", 2, 0, 0, half, half), half * row_bytes, relay[1:], 0)]

    def rows(part):
        return (0, SHARE) if part is None else part

    states = {}
    for d in (3, 1, 2):
        got = ring(sends, "x", N_ROW, lambda dx, part: ("S", d, dx, 0, *rows(part)),
                   lambda part: ("S", d, 0, 0, *rows(part)), ((0, half), (half, half)), SHARE * row_bytes, come[d], 0)
        got[0] = come[d]
        states[d] = [k for dx in range(N_ROW) for k in got[dx]]
        for dx in (0, 3, 1, 2):
            k = add("s", ("S", d, dx, 0, 0, SHARE), ("S", d, dx, 0, 0, SHARE), SHARE * row_bytes, got[dx], 5)
            states[d].append(k)

    def cent(part):
        return (0, CENT) if part is None else part

    halves = ((0, CENT // 2), (CENT // 2, CENT // 2))
    centres = ring(sends, "y", N_SA, lambda d, part: ("F", d, *cent(part)), lambda part: ("F", 0, *cent(part)), halves,
                   CENT * row_bytes, ("local", *relay), 3)
    tasks.append((("distance", 0), ("local",), 0.8))
    for d in (3, 1, 2):
        tasks.append((("distance", d), tuple(states[d] + centres[d]), 0.8))
    return sends, tasks


def spread_plan():
    sends = []

    def cut(cols, half):
        first, rows = (0, CENT) if half is None else half
        return (first, rows, cols[0], cols[1] - cols[0])

    halves = ((0, CENT // 2), (CENT // 2, CENT // 2))

    def area(cols):
        return 2 * CENT * (cols[1] - cols[0])

    def r_ring(axis, size, place, cols, deps, rank):
        return ring(sends, axis, size, lambda d, half: ("R", *place(d), 0, cut(cols, half)),
                    lambda half: ("R", *place(0), 0, cut(cols, half)), halves, area(cols), deps, rank)

    y_own = r_ring("y", N_SA, lambda d: (d, 0), EVERY, (), 0)
    z_own = r_ring("z", N_Z, lambda d: (0, d), Z_FIRST, (), 0)
    arrived = {}
    for dz in range(1, N_Z):
        arrived[0, dz, Z_FIRST] = z_own[dz]
        got = r_ring("y", N_SA, lambda d: (d, dz), Z_FIRST, z_own[dz], 10)
        for dy in range(1, N_SA):
            arrived[dy, dz, Z_FIRST] = got[dy]
    in_r, in_c = {(dy, 0): list(y_own[dy]) if dy else [] for dy in range(N_SA)}, {}
    for dy in range(N_SA):
        need = in_r[dy, 0]
        got = r_ring("z", N_Z, lambda d: (dy, d), Y_FIRST, need, 10)
        for dz in range(1, N_Z):
            arrived[dy, dz, Y_FIRST] = got[dz]
        got = ring(sends, "x", N_ROW, lambda d, half: ("C", dy, d, cut(EVERY, half)),
                   lambda half: ("R", dy, 0, 0, cut(EVERY, half)), halves, area(EVERY), need, 20)
        in_c[dy] = [k for ks in got.values() for k in ks] + need
        sends.append(Send("s", ("R", dy, 0, 0, cut(EVERY, None)), ("R", dy, 0, 1, cut(EVERY, None)), area(EVERY), need, 30))
        in_r[dy, 1] = [len(sends) - 1]
    for (dy, dz, cols), need in arrived.items():
        sends.append(Send("s", ("R", dy, dz, 0, cut(cols, None)), ("R", dy, dz, 1, cut(cols, None)), area(cols), need, 30))
        in_r.setdefault((dy, dz * 2), []).extend(need)
        in_r.setdefault((dy, dz * 2 + 1), []).append(len(sends) - 1)

    tasks = []
    for dy in range(N_SA):
        tasks.append((("columns", dy), tuple(in_c[dy]), 0.15))
    for group in GROUPS:
        for dy in range(N_SA):
            need = [k for slot in group for k in in_r[dy, slot]] + in_c[dy]
            tasks.append((("right", (group, dy)), tuple(need), 0.5))
            tasks.append((("left", (group, dy)), tuple(need), 0.5))
    return sends, tasks


def timetable(sends, tasks, local):
    free, pending, done, queue, steps = {}, set(range(len(sends))), set(), [], []
    undone = list(range(len(tasks)))
    relayed = {d for send in sends for d in send.deps}

    def start_ready(now):
        ready = sorted((k for k in pending if all(d in done for d in sends[k].deps)), key=lambda k: (sends[k].rank, k))
        for k in ready:
            pending.discard(k)
            link = sends[k].link
            free[link] = max(now, free.get(link, 0.0)) + sends[k].size / RATE.get(link, LINK_RATE)
            heapq.heappush(queue, (free[link] + LATENCY + (0.0 if k in relayed or local is not None else LEAF), k))
            steps.append(("start", k))

    core = 0.0
    start_ready(core)
    if local is not None:
        core += local
        steps.append(("local", None))
        done.add("local")
        start_ready(core)
    while queue or undone:
        coming = queue[0][0] if queue else math.inf
        ready = [t for t in undone if all(d in done for d in tasks[t][1])]
        if ready and coming - core >= 0.6 * tasks[ready[0]][2]:
            undone.remove(ready[0])
            core += tasks[ready[0]][2]
            steps.append(("task", tasks[ready[0]][0]))
            continue
        now, k = heapq.heappop(queue)
        core = max(core, now)
        done.add(k)
        steps.append(("wait", k))
        start_ready(core)
    return steps, core


def left_place(dev, half, slot, slot_half):
    return (dev * 2 + half) * 2 * N_COL + slot * 2 + slot_half


def right_place(slot, half, place):
    return 2 * N_ROW * 2 * N_COL + (slot * 2 + half) * 2 * N_ROW + place


def normal_kernel(plans, steps, table, pick, states, pool, o_ref, r_all, c_all, blocks, cq, rq, s_all, f_all, relay,
                  pool_local, inner, sample_norms, centre_norms, place_of, copy_sems, first_out, first_in, out_sems,
                  in_sems):
    y, x, col = lax.axis_index("sa"), lax.axis_index("row"), lax.axis_index("col")
    z, core = col // 2, col % 2
    to = {
        "y+": {"sa": (y + 1) % N_SA},
        "y-": {"sa": (y + 3) % N_SA},
        "x+": {"row": (x + 1) % N_ROW},
        "x-": {"row": (x + 3) % N_ROW},
        "z+": {"col": (z + 1) % N_Z * 2 + core},
        "z-": {"col": (z + 7) % N_Z * 2 + core},
        "s": {"col": z * 2 + 1 - core},
    }
    mesh_id = pl.DeviceIdType.MESH
    pool_copy = pltpu.make_async_copy(pool, pool_local, copy_sems.at[0])
    pool_copy.start()
    states_copy = pltpu.make_async_copy(
        states.at[pl.ds(pl.multiple_of(y * COUNT, COUNT), COUNT), :], s_all.at[0], copy_sems.at[1])
    states_copy.start()
    barrier = pltpu.get_barrier_semaphore()
    for peer in to.values():
        pl.semaphore_signal(barrier, inc=1, device_id=peer, device_id_type=mesh_id)
    pl.semaphore_wait(barrier, len(to))

    def place_ref(place):
        kind = place[0]
        if kind == "H":
            first = (y + place[1]) % N_SA * COUNT + (x * 2 + core) * SHARE + place[2]
            return states.at[pl.ds(pl.multiple_of(first, 8), place[3]), :]
        if kind == "B":
            return relay.at[place[1]]
        if kind == "S":
            first = ((x + place[2]) % N_ROW * 2 + core) * SHARE + place[4]
            return s_all.at[place[1], pl.ds(pl.multiple_of(first, 8), place[5]), :]
        if kind == "F":
            return f_all.at[place[1], pl.ds(place[2], place[3]), :]
        first, rows, start, count = place[-1]
        rows, cols = pl.ds(first, rows), pl.ds(place[1] * COUNT + start, count)
        if kind == "R":
            return r_all.at[place[2] * 2 + place[3], rows, cols]
        return c_all.at[place[2] - 1, rows, cols]

    def landing(send):
        if send.src[0] == "S":
            return place_ref(send.src)
        return place_ref(send.dst)

    def copies_of(sends, out, into):
        return [
            pltpu.make_async_remote_copy(
                src_ref=place_ref(send.src), dst_ref=landing(send), send_sem=out.at[k], recv_sem=into.at[k],
                device_id=to[send.link], device_id_type=mesh_id)
            for k, send in enumerate(sends)
        ]

    def dot(left, right, precision=None):
        return lax.dot_general(left, right, (((1,), (1,)), ((), ())), precision=precision,
                               preferred_element_type=jnp.float32)

    def distance(d):
        sample, centre = s_all[d], f_all[d]
        cross = dot(centre, sample, lax.Precision.HIGHEST)
        squares = sample * sample
        squares = squares[:, :MB] + squares[:, MB:]
        norms = jnp.sum(squares.T, axis=0, keepdims=True)
        own = jnp.sum(centre * centre, axis=1, keepdims=True)
        if d:
            inner[...] += cross
            sample_norms[...] += norms
            centre_norms[...] += own
        else:
            inner[...], sample_norms[...], centre_norms[...] = cross, norms, own

    def local():
        pool_copy.wait()

        @pl.loop(0, CENT // 8)
        def _(m):
            for n in range(8):
                f_all[0, m * 8 + n] = pool_local[pick[m * 8 + n] & (POOL_DEV - 1)]

        states_copy.wait()

    def column(dev):
        return c_all.at[dev - 1] if dev else r_all.at[0]

    def quarter(half):
        return pl.ds(pl.multiple_of(half * MB + y * QUART, QUART), QUART)

    begun = set()

    def put(where, value, key):
        if key in begun:
            blocks[where] += value
        else:
            blocks[where] = value

    def task(kind, what):
        if kind == "distance":
            distance(what)
            return
        if kind == "columns":
            cols = slice(what * COUNT, (what + 1) * COUNT)
            for dev in range(N_ROW):
                for half in range(2):
                    top = (dev * 2 + half) * QUART
                    cq[top:top + QUART, cols] = column(dev)[quarter(half), cols]
            return
        group, dy = what
        cols = slice(dy * COUNT, (dy + 1) * COUNT)
        if kind == "right":
            for slot in group:
                got = dot(cq[:, cols], r_all[slot, :, cols])
                for half in range(2):
                    for n in range(2 * N_ROW):
                        put(right_place(slot, half, n), got[n * QUART:(n + 1) * QUART, half * MB:(half + 1) * MB],
                            (kind, group))
        else:
            for n, slot in enumerate(group):
                for half in range(2):
                    top = (n * 2 + half) * QUART
                    rq[top:top + QUART, :] = r_all[slot, quarter(half), cols]
            for dev in range(N_ROW):
                got = dot(rq[...], column(dev)[:, cols])
                for half in range(2):
                    for n in range(8):
                        put(left_place(dev, half, group[n // 2], n % 2),
                            got[n * QUART:(n + 1) * QUART, half * MB:(half + 1) * MB], (kind, group))
        begun.add((kind, group))

    def run(copies, order):
        for kind, what in order:
            if kind == "wait":
                copies[what].wait_recv()
            elif kind == "start":
                copies[what].start()
            elif kind == "local":
                local()
            else:
                task(*what)

    first = copies_of(plans[0], first_out, first_in)
    run(first, steps[0])
    total = sample_norms[...] + centre_norms[...] - 2.0 * inner[...]
    r_all[0, :, :COUNT] = jnp.exp((2.0 * F - total) / (4.0 * math.sqrt(F))).astype(jnp.bfloat16)
    second = copies_of(plans[1], out_sems, in_sems)
    for kind, what in steps[1]:
        if kind != "start":
            break
        second[what].start()
    for copy in first:
        copy.wait_send()

    @pl.loop(0, o_ref.shape[0] // 3)
    def _(m):
        for n in range(3):
            k = m * 3 + n
            i, j = table[0, k], table[1, k]
            row_i, col_i, half_i = i >> 5, (i >> 1) & 15, i & 1
            row_j, col_j, half_j = j >> 5, (j >> 1) & 15, j & 1

            def far_col(c):
                return (((c >> 1) - z) & 7) * 2 + ((c + core) & 1)

            left = left_place((row_j - x) & 3, half_j, far_col(col_i), half_i)
            right = right_place(far_col(col_j), half_j, ((row_i - x) & 3) * 2 + half_i)
            straight = jnp.logical_and(row_i == x, col_j == col)
            place_of[k] = right + (left - right) * straight.astype(jnp.int32)

    begin = [k for k, (kind, _) in enumerate(steps[1]) if kind != "start"][0]
    run(second, steps[1][begin:])
    for copy in second:
        copy.wait_send()

    @pl.loop(0, o_ref.shape[0] // 3)
    def _(m):
        for n in range(3):
            k = m * 3 + n
            o_ref[k] = blocks[place_of[k]] * (1.0 / (N_SA * COUNT))


def normal_tiles(table, pick, states, pool):
    first, first_tasks = gather_inputs_plan()
    second, second_tasks = spread_plan()
    steps = [timetable(first, first_tasks, 1.5)[0], timetable(second, second_tasks, None)[0]]
    whole = N_SA * COUNT
    smem, anywhere = pl.BlockSpec(memory_space=pltpu.SMEM), pl.BlockSpec(memory_space=pl.ANY)
    return pl.pallas_call(
        functools.partial(normal_kernel, [first, second], steps),
        out_shape=jax.ShapeDtypeStruct((table.shape[1], QUART, MB), jnp.float32),
        in_specs=[smem, smem, anywhere, anywhere],
        out_specs=pl.BlockSpec(memory_space=pltpu.VMEM),
        scratch_shapes=[
            pltpu.VMEM((N_COL, CENT, whole), jnp.bfloat16),
            pltpu.VMEM((N_ROW - 1, CENT, whole), jnp.bfloat16),
            pltpu.VMEM((2 * 2 * N_ROW * 2 * N_COL, QUART, MB), jnp.float32),
            pltpu.VMEM((CENT, whole), jnp.bfloat16),
            pltpu.VMEM((CENT, COUNT), jnp.bfloat16),
            pltpu.VMEM((N_SA, COUNT, FEAT), jnp.float32),
            pltpu.VMEM((N_SA, CENT, FEAT), jnp.float32),
            pltpu.VMEM((2, SHARE // 2, FEAT), jnp.float32),
            pltpu.VMEM(pool.shape, jnp.float32),
            pltpu.VMEM((CENT, COUNT), jnp.float32),
            pltpu.VMEM((1, COUNT), jnp.float32),
            pltpu.VMEM((CENT, 1), jnp.float32),
            pltpu.SMEM((table.shape[1],), jnp.int32),
            pltpu.SemaphoreType.DMA((2,)),
            pltpu.SemaphoreType.DMA((len(first),)),
            pltpu.SemaphoreType.DMA((len(first),)),
            pltpu.SemaphoreType.DMA((len(second),)),
            pltpu.SemaphoreType.DMA((len(second),)),
        ],
        compiler_params=pltpu.CompilerParams(
            collective_id=0, has_side_effects=True, vmem_limit_bytes=56 * 2**20
        ),
    )(table, pick, states, pool)


def shards(states, pool, pick, tile_table):
    return normal_tiles(tile_table.T, pick, states, pool)


def solution(mesh):
    placed = (P(None, "sa"), P(("row", "col"), "sa"), P(("row", "col")), P(("row", "col"), None))
    return jax.shard_map(
        shards, mesh=mesh, in_specs=placed, out_specs=P(("row", "col"), "sa", None), check_vma=False
    )
```

```python
import functools
import heapq
import math

import jax
import jax.numpy as jnp
from jax import lax
from jax.experimental import pallas as pl
from jax.experimental.pallas import tpu as pltpu
from jax.sharding import PartitionSpec as P

F = 1024
M = 16384
MB = 128
N_SA = 4
N_ROW = 4
N_COL = 16
N_Z = 8
QUART = MB // N_SA
CENT = 256
COUNT = 640
POOL_DEV = 512
FEAT = F // N_SA
SPLIT = 384
Z_FIRST = (0, SPLIT)
Y_FIRST = (SPLIT, COUNT)
EVERY = (0, COUNT)
WINDOWS = (Z_FIRST, Y_FIRST)
PIECES = 3
GROUPS = ((0, 1, 2, 14), (3, 15, 4, 12), (5, 13, 6, 10), (7, 11, 8, 9))
RATE = {"s": 300e3}
LINK_RATE = 45e3
LATENCY = 1.7
LEAF = 3.0


class Send:
    def __init__(self, link, src, dst, size, deps, rank):
        self.link, self.src, self.dst, self.size = link, src, dst, size
        self.deps, self.rank = tuple(deps), rank


def ring(sends, axis, size, unit, own, halves, nbytes, deps, rank):
    filled = {}
    for sign, half in (("+", halves[0]), ("-", halves[1])):
        step = -1 if sign == "+" else 1
        need, at = deps, 0
        for hop in range(1, size // 2 + 1):
            last = hop == size // 2
            part = half if last else None
            to = (at + step) % size
            src = own(part) if at == 0 else unit(at, part)
            sends.append(Send(axis + sign, src, unit(to, part), nbytes // 2 if last else nbytes, need, rank + hop))
            filled.setdefault(to, []).append(len(sends) - 1)
            need, at = [len(sends) - 1], to
    return filled


def share_of(w):
    return (WINDOWS[w][1] - WINDOWS[w][0]) // 8


def inputs_plan(sends, tasks):
    row_bytes = 4 * FEAT

    def add(*args):
        sends.append(Send(*args))
        return len(sends) - 1

    relays = []
    for w in range(2):
        half = share_of(w) // 2
        relays.append(add("y+", ("H", 2, w, 0, half), ("B", 2 * w, half), half * row_bytes, (), 0))
        relays.append(add("y-", ("H", 2, w, half, half), ("B", 2 * w + 1, half), half * row_bytes, (), 0))
    states = {}
    for w in range(2):
        share = share_of(w)
        half = share // 2
        come = {3: [add("y+", ("H", 1, w, 0, share), ("S", 3, 0, w, 0, share), share * row_bytes, (), 1 + w)],
                1: [add("y-", ("H", 3, w, 0, share), ("S", 1, 0, w, 0, share), share * row_bytes, (), 1 + w)]}
        come[2] = [add("y+", ("B", 2 * w, half), ("S", 2, 0, w, 0, half), half * row_bytes, [relays[2 * w]], 0),
                   add("y-", ("B", 2 * w + 1, half), ("S", 2, 0, w, half, half), half * row_bytes, [relays[2 * w + 1]], 0)]

        def rows(part):
            return (0, share) if part is None else part

        for d in (3, 1, 2):
            got = ring(sends, "x", N_ROW, lambda dx, part: ("S", d, dx, w, *rows(part)),
                       lambda part: ("S", d, 0, w, *rows(part)), ((0, half), (half, half)), share * row_bytes, come[d], 0)
            got[0] = come[d]
            states[d, w] = [k for dx in range(N_ROW) for k in got[dx]]
            for dx in (0, 3, 1, 2):
                place = ("S", d, dx, w, 0, share)
                states[d, w].append(add("s", place, place, share * row_bytes, got[dx], 5))

    def cent(part):
        return (0, CENT) if part is None else part

    halves = ((0, CENT // 2), (CENT // 2, CENT // 2))
    centres = ring(sends, "y", N_SA, lambda d, part: ("F", d, *cent(part)), lambda part: ("F", 0, *cent(part)), halves,
                   CENT * row_bytes, ("local", *relays), 3)
    tasks.append(("local", None, (), 1.5, True))
    for w in range(2):
        tasks.append(("distance", (0, w), ("local",), 0.5, False))
    for n in range(PIECES):
        tasks.append(("places", n, ("local",), 0.8, False))
    for w in range(2):
        for d in (3, 1, 2):
            need = (*states[d, w], *centres[d], *([("kernel", 0)] if w else []))
            tasks.append(("distance", (d, w), need, 0.5, True))
        tasks.append(("kernel", w, tuple(("distance", (d, w)) for d in range(N_SA)), 0.3, True))


def spread_plan(sends, tasks):
    kernels = [("kernel", w) for w in range(2)]

    def cut(cols, half):
        first, rows = (0, CENT) if half is None else half
        return (first, rows, cols[0], cols[1] - cols[0])

    halves = ((0, CENT // 2), (CENT // 2, CENT // 2))

    def area(cols):
        return 2 * CENT * (cols[1] - cols[0])

    def r_ring(axis, size, place, cols, deps, rank):
        return ring(sends, axis, size, lambda d, half: ("R", *place(d), 0, cut(cols, half)),
                    lambda half: ("R", *place(0), 0, cut(cols, half)), halves, area(cols), deps, rank)

    z_own = r_ring("z", N_Z, lambda d: (0, d), Z_FIRST, kernels[:1], 6)
    y_own = [r_ring("y", N_SA, lambda d: (d, 0), WINDOWS[w], kernels[w:w + 1], 6) for w in range(2)]
    arrived = {}
    for dz in range(1, N_Z):
        arrived[0, dz, Z_FIRST] = z_own[dz]
        got = r_ring("y", N_SA, lambda d: (d, dz), Z_FIRST, z_own[dz], 10)
        for dy in range(1, N_SA):
            arrived[dy, dz, Z_FIRST] = got[dy]
    in_r, in_c = {(dy, 0): y_own[0][dy] + y_own[1][dy] if dy else kernels for dy in range(N_SA)}, {}
    for dy in range(N_SA):
        need = in_r[dy, 0]
        got = r_ring("z", N_Z, lambda d: (dy, d), Y_FIRST, y_own[1][dy] if dy else kernels[1:], 10)
        for dz in range(1, N_Z):
            arrived[dy, dz, Y_FIRST] = got[dz]
        got = ring(sends, "x", N_ROW, lambda d, half: ("C", dy, d, cut(EVERY, half)),
                   lambda half: ("R", dy, 0, 0, cut(EVERY, half)), halves, area(EVERY), need, 20)
        in_c[dy] = [k for ks in got.values() for k in ks] + need
        sends.append(Send("s", ("R", dy, 0, 0, cut(EVERY, None)), ("R", dy, 0, 1, cut(EVERY, None)), area(EVERY), need, 30))
        in_r[dy, 1] = [len(sends) - 1]
    for (dy, dz, cols), need in arrived.items():
        halved = dz == N_Z // 2 if dy == 0 or cols == Y_FIRST else dy == N_SA // 2
        for k in need if halved else [None]:
            part = cut(cols, None) if k is None else sends[k].dst[-1]
            size = area(cols) if k is None else sends[k].size
            sends.append(Send("s", ("R", dy, dz, 0, part), ("R", dy, dz, 1, part), size, need if k is None else [k], 30))
            in_r.setdefault((dy, dz * 2 + 1), []).append(len(sends) - 1)
        in_r.setdefault((dy, dz * 2), []).extend(need)

    for dy in range(N_SA):
        tasks.append(("columns", dy, tuple(in_c[dy]), 0.15, False))
    for group in GROUPS:
        for dy in range(N_SA):
            need = [k for slot in group for k in in_r[dy, slot]] + in_c[dy]
            tasks.append(("right", (group, dy), (*need, ("columns", dy)), 0.5, False))
            tasks.append(("left", (group, dy), tuple(need), 0.5, False))


def timetable(sends, tasks):
    free, pending, done, queue, steps = {}, set(range(len(sends))), set(), [], []
    undone = list(range(len(tasks)))
    relayed = {d for send in sends for d in send.deps} | {d for t in tasks if t[4] for d in t[2]}

    def start_ready(now):
        ready = sorted((k for k in pending if all(d in done for d in sends[k].deps)), key=lambda k: (sends[k].rank, k))
        for k in ready:
            pending.discard(k)
            link = sends[k].link
            free[link] = max(now, free.get(link, 0.0)) + sends[k].size / RATE.get(link, LINK_RATE)
            heapq.heappush(queue, (free[link] + LATENCY + (0.0 if k in relayed else LEAF), k))
            steps.append(("start", k))

    core = 0.0
    start_ready(core)
    while queue or undone:
        coming = queue[0][0] if queue else math.inf
        ready = [t for t in undone if all(d in done for d in tasks[t][2])]
        ready.sort(key=lambda t: not tasks[t][4])
        if ready and coming - core >= (0.0 if tasks[ready[0]][4] else 0.3 * tasks[ready[0]][3]):
            kind, what, _, span, _ = tasks[ready[0]]
            undone.remove(ready[0])
            core += span
            steps.append((kind, what))
            done.add(kind if what is None else (kind, what))
            start_ready(core)
            continue
        now, k = heapq.heappop(queue)
        core = max(core, now)
        done.add(k)
        steps.append(("wait", k))
        start_ready(core)
    return steps, core


def left_place(dev, half, slot, slot_half):
    return (dev * 2 + half) * 2 * N_COL + slot * 2 + slot_half


def right_place(slot, half, place):
    return 2 * N_ROW * 2 * N_COL + (slot * 2 + half) * 2 * N_ROW + place


def normal_kernel(sends, steps, table, pick, states, pool, out, r_all, c_all, blocks, cq, rq, s_all, f_all, relay,
                  pool_local, inner, centre_norms, place_of, o_ref, copy_sems, out_sems, in_sems):
    y, x, col = lax.axis_index("sa"), lax.axis_index("row"), lax.axis_index("col")
    z, core = col // 2, col % 2
    to = {
        "y+": {"sa": (y + 1) % N_SA},
        "y-": {"sa": (y + 3) % N_SA},
        "x+": {"row": (x + 1) % N_ROW},
        "x-": {"row": (x + 3) % N_ROW},
        "z+": {"col": (z + 1) % N_Z * 2 + core},
        "z-": {"col": (z + 7) % N_Z * 2 + core},
        "s": {"col": z * 2 + 1 - core},
    }
    mesh_id = pl.DeviceIdType.MESH
    pool_copy = pltpu.make_async_copy(pool, pool_local, copy_sems.at[0])
    pool_copy.start()
    states_copy = pltpu.make_async_copy(
        states.at[pl.ds(pl.multiple_of(y * COUNT, COUNT), COUNT), :], s_all.at[0], copy_sems.at[1])
    states_copy.start()
    barrier = pltpu.get_barrier_semaphore()
    for peer in to.values():
        pl.semaphore_signal(barrier, inc=1, device_id=peer, device_id_type=mesh_id)
    pl.semaphore_wait(barrier, len(to))

    def place_ref(place):
        kind = place[0]
        if kind == "H":
            w = place[2]
            first = (y + place[1]) % N_SA * COUNT + WINDOWS[w][0] + (x * 2 + core) * share_of(w) + place[3]
            return states.at[pl.ds(pl.multiple_of(first, 8), place[4]), :]
        if kind == "B":
            return relay.at[place[1], pl.ds(0, place[2]), :]
        if kind == "S":
            w = place[3]
            first = WINDOWS[w][0] + ((x + place[2]) % N_ROW * 2 + core) * share_of(w) + place[4]
            return s_all.at[place[1], pl.ds(pl.multiple_of(first, 8), place[5]), :]
        if kind == "F":
            return f_all.at[place[1], pl.ds(place[2], place[3]), :]
        first, rows, start, count = place[-1]
        rows, cols = pl.ds(first, rows), pl.ds(place[1] * COUNT + start, count)
        if kind == "R":
            return r_all.at[place[2] * 2 + place[3], rows, cols]
        return c_all.at[place[2] - 1, rows, cols]

    def landing(send):
        if send.src[0] == "S":
            return place_ref(send.src)
        return place_ref(send.dst)

    copies = [
        pltpu.make_async_remote_copy(
            src_ref=place_ref(send.src), dst_ref=landing(send), send_sem=out_sems.at[k], recv_sem=in_sems.at[k],
            device_id=to[send.link], device_id_type=mesh_id)
        for k, send in enumerate(sends)
    ]

    def dot(left, right, precision=None):
        return lax.dot_general(left, right, (((1,), (1,)), ((), ())), precision=precision,
                               preferred_element_type=jnp.float32)

    begun = set()

    def put(ref, where, value, key):
        if key in begun:
            ref[where] += value
        else:
            ref[where] = value

    def distance(d, w):
        cols = slice(*WINDOWS[w])
        sample, centre = s_all[d, cols, :], f_all[d]
        squares = sample * sample
        squares = squares[:, :MB] + squares[:, MB:]
        norms = jnp.sum(squares.T, axis=0, keepdims=True)
        cross = dot(centre, sample, lax.Precision.HIGHEST)
        put(inner, (slice(None), cols), norms - 2.0 * cross, w)
        begun.add(w)
        if ("centre", d) not in begun:
            own = jnp.sum(centre * centre, axis=1, keepdims=True)
            put(centre_norms, (slice(None), slice(None)), own, "centres")
            begun.update(("centres", ("centre", d)))

    def kernel_values(w):
        cols = slice(*WINDOWS[w])
        total = inner[:, cols] + centre_norms[...]
        r_all[0, :, cols] = jnp.exp((2.0 * F - total) / (4.0 * math.sqrt(F))).astype(jnp.bfloat16)

    def places(piece):
        size = out.shape[0] // PIECES

        @pl.loop(0, size)
        def _(m):
            k = piece * size + m
            i, j = table[0, k], table[1, k]
            row_i, col_i, half_i = i >> 5, (i >> 1) & 15, i & 1
            row_j, col_j, half_j = j >> 5, (j >> 1) & 15, j & 1

            def far_col(c):
                return (((c >> 1) - z) & 7) * 2 + ((c + core) & 1)

            left = left_place((row_j - x) & 3, half_j, far_col(col_i), half_i)
            right = right_place(far_col(col_j), half_j, ((row_i - x) & 3) * 2 + half_i)
            straight = jnp.logical_and(row_i == x, col_j == col)
            place_of[k] = right + (left - right) * straight.astype(jnp.int32)

    def local():
        pool_copy.wait()

        @pl.loop(0, CENT // 8)
        def _(m):
            for n in range(8):
                f_all[0, m * 8 + n] = pool_local[pick[m * 8 + n] & (POOL_DEV - 1)]

        states_copy.wait()

    def column(dev):
        return c_all.at[dev - 1] if dev else r_all.at[0]

    def quarter(half):
        return pl.ds(pl.multiple_of(half * MB + y * QUART, QUART), QUART)

    def task(kind, what):
        if kind == "columns":
            cols = slice(what * COUNT, (what + 1) * COUNT)
            for dev in range(N_ROW):
                for half in range(2):
                    top = (dev * 2 + half) * QUART
                    cq[top:top + QUART, cols] = column(dev)[quarter(half), cols]
            return
        group, dy = what
        cols = slice(dy * COUNT, (dy + 1) * COUNT)
        if kind == "right":
            for slot in group:
                got = dot(cq[:, cols], r_all[slot, :, cols])
                for half in range(2):
                    for n in range(2 * N_ROW):
                        put(blocks, right_place(slot, half, n), got[n * QUART:(n + 1) * QUART, half * MB:(half + 1) * MB],
                            (kind, group))
        else:
            for n, slot in enumerate(group):
                for half in range(2):
                    top = (n * 2 + half) * QUART
                    rq[top:top + QUART, :] = r_all[slot, quarter(half), cols]
            for dev in range(N_ROW):
                got = dot(rq[...], column(dev)[:, cols])
                for half in range(2):
                    for n in range(8):
                        put(blocks, left_place(dev, half, group[n // 2], n % 2),
                            got[n * QUART:(n + 1) * QUART, half * MB:(half + 1) * MB], (kind, group))
        begun.add((kind, group))

    for kind, what in steps:
        if kind == "wait":
            copies[what].wait_recv()
        elif kind == "start":
            copies[what].start()
        elif kind == "local":
            local()
        elif kind == "distance":
            distance(*what)
        elif kind == "kernel":
            kernel_values(what)
        elif kind == "places":
            places(what)
        else:
            task(kind, what)

    size = out.shape[0] // PIECES
    results = []
    for piece in range(PIECES):
        @pl.loop(0, size)
        def _(m):
            k = piece * size + m
            o_ref[k] = blocks[place_of[k]] * (1.0 / (N_SA * COUNT))

        part = pl.ds(piece * size, size)
        results.append(pltpu.make_async_copy(o_ref.at[part], out.at[part], copy_sems.at[2 + piece]))
        results[-1].start()
    for copy in copies:
        copy.wait_send()
    for copy in results:
        copy.wait()


def normal_tiles(table, pick, states, pool):
    sends, tasks = [], []
    inputs_plan(sends, tasks)
    spread_plan(sends, tasks)
    steps, _ = timetable(sends, tasks)
    whole = N_SA * COUNT
    smem, anywhere = pl.BlockSpec(memory_space=pltpu.SMEM), pl.BlockSpec(memory_space=pl.ANY)
    return pl.pallas_call(
        functools.partial(normal_kernel, sends, steps),
        out_shape=jax.ShapeDtypeStruct((table.shape[1], QUART, MB), jnp.float32),
        in_specs=[smem, smem, anywhere, anywhere],
        out_specs=anywhere,
        scratch_shapes=[
            pltpu.VMEM((N_COL, CENT, whole), jnp.bfloat16),
            pltpu.VMEM((N_ROW - 1, CENT, whole), jnp.bfloat16),
            pltpu.VMEM((2 * 2 * N_ROW * 2 * N_COL, QUART, MB), jnp.float32),
            pltpu.VMEM((CENT, whole), jnp.bfloat16),
            pltpu.VMEM((CENT, COUNT), jnp.bfloat16),
            pltpu.VMEM((N_SA, COUNT, FEAT), jnp.float32),
            pltpu.VMEM((N_SA, CENT, FEAT), jnp.float32),
            pltpu.VMEM((4, share_of(0) // 2, FEAT), jnp.float32),
            pltpu.VMEM(pool.shape, jnp.float32),
            pltpu.VMEM((CENT, COUNT), jnp.float32),
            pltpu.VMEM((CENT, 1), jnp.float32),
            pltpu.SMEM((table.shape[1],), jnp.int32),
            pltpu.VMEM((table.shape[1], QUART, MB), jnp.float32),
            pltpu.SemaphoreType.DMA((2 + PIECES,)),
            pltpu.SemaphoreType.DMA((len(sends),)),
            pltpu.SemaphoreType.DMA((len(sends),)),
        ],
        compiler_params=pltpu.CompilerParams(
            collective_id=0, has_side_effects=True, vmem_limit_bytes=56 * 2**20
        ),
    )(table, pick, states, pool)


def shards(states, pool, pick, tile_table):
    return normal_tiles(tile_table.T, pick, states, pool)


def solution(mesh):
    placed = (P(None, "sa"), P(("row", "col"), "sa"), P(("row", "col")), P(("row", "col"), None))
    return jax.shard_map(
        shards, mesh=mesh, in_specs=placed, out_specs=P(("row", "col"), "sa", None), check_vma=False
    )
```
